128 devices in a mesh: ctx: 8 (over x_hi, z), head: 16 (over y, x_lo, core).
Axes of the slice: x: 4 (x_hi: 2, x_lo: 2; x = x_hi * 2 + x_lo), y: 4, z: 4, core: 2. Of those that a mesh axis runs over, the one named last changes fastest.
Arguments:
- hyena_query: bfloat16 [4096, 8192], P('ctx', 'head'), may hold values from -6 to 6
- hyena_key: bfloat16 [4096, 8192], P('ctx', 'head'), may hold values from -6 to 6
- hyena_value: bfloat16 [4096, 8192], P('ctx', 'head'), may hold values from -6 to 6
- hyena_filter: bfloat16 [128, 8192], P(None, 'head'), may hold values from -0.5 to 0.5
- attn_query: bfloat16 [4096, 8192], P('ctx', 'head'), may hold values from -100 to 100
- attn_key: bfloat16 [4096, 8192], P('ctx', 'head'), may hold values from -4 to 4
- attn_value: bfloat16 [4096, 8192], P('ctx', 'head'), may hold values from -12 to 12
- segment_ids: int32 [4096], replicated, may hold values from 0 to 5, never falling along the last dimension, each value on 1 to 2048 neighbouring positions
- out_weight: bfloat16 [8192, 8192], P('head'), may hold values from -0.09375 to 0.09375
Outputs:
- hyena_out: bfloat16 [4096, 8192], P('ctx', 'head')
- stream: bfloat16 [4096, 8192], P('ctx', 'head')
The draws below stay inside these ranges and needn't reach their ends.
Inputs may be any that keep to these rules, and one draw needn't show every extreme that they name: `segment_ids`: never falls along the positions; each document is 1 to 2048 positions in a row, one exactly 2048.
All inputs are finite; a program needn't handle non-finite values.
Results may differ from the reference program's by a relative error of at most 0.014.
Values may be sent and summed in bfloat16 or wider, within the bound.
No kernel may reach another device: no remote copies, remote signals or barrier semaphores. Data moves between devices by JAX's collectives and lax.ppermute only.
A program may use at most 320 MiB of HBM per device.

```python
import math
import jax
import jax.numpy as jnp
import numpy as np
from jax import lax

D = 8192
HEADS = 64
HEAD_DIM = 128
FILT = 128
SEGS = 6
LENGTH = 4096
N_HEAD = 16


def shared_pair(key):
    base_query = jax.random.truncated_normal(jax.random.fold_in(key, 11), -4.0, 4.0, (LENGTH, D), jnp.float32)
    base_key = jax.random.truncated_normal(jax.random.fold_in(key, 12), -4.0, 4.0, (LENGTH, D), jnp.float32)
    query_out = base_query
    key_out = base_key
    return (query_out, key_out)


def draw_attn_query(key, part):
    return shared_pair(key)[0].astype(jnp.bfloat16)


def draw_attn_key(key, part):
    return shared_pair(key)[1].astype(jnp.bfloat16)


def with_spikes(result, key, source, target, shards_of, factor):
    def block_of(axis_at):
        return (jnp.arange(result.shape[axis_at]) // (result.shape[axis_at] // shards_of)).reshape((-1,) + (1,) * (result.ndim - 1 - axis_at))

    first = jax.random.permutation(key, shards_of)[block_of(target)]
    far = (block_of(target) + shards_of // 2) % shards_of
    return jnp.where((block_of(source) == first) | (block_of(source) == far), factor * result, result)


def block_scale(stream_key, dims, cuts, least, high):
    gain = 1.0
    for axis_at, blocks in cuts:
        steps = jax.random.uniform(jax.random.fold_in(jax.random.fold_in(stream_key, 6), axis_at), (blocks,), jnp.float32, least / len(cuts), high / len(cuts))
        gain = gain * jnp.repeat(jnp.exp(steps), dims[axis_at] // blocks).reshape((-1,) + (1,) * (len(dims) - 1 - axis_at))
    return gain


def profile(number_of, total, bound, lean):
    portions = [(1 << 20) // math.isqrt(standing ** lean) + 1 for standing in range(2, number_of + 1)]
    rest, holding = total - bound - (number_of - 1), [1] * (number_of - 1)
    while rest > 0:
        free = [i for i in range(number_of - 1) if holding[i] < bound]
        whole, budget = sum([portions[i] for i in free]), rest
        for i in free:
            more = min(bound - holding[i], max(1, budget * portions[i] // whole), rest)
            holding[i] = holding[i] + more
            rest = rest - more
    return np.array([bound] + holding)


def ragged_sizes(stream_key, amount, total, most, lean):
    if amount == 2:
        one = jax.random.randint(stream_key, (), max(1, total - most), min(most, total - 1) + 1)
        return jnp.stack([one, total - one])
    tallies = jnp.asarray(profile(amount, total, most, lean), jnp.int32)
    couples = (amount - 1) // 2
    source_of, sink = tallies[1:1 + 2 * couples:2], tallies[2:2 + 2 * couples:2]
    room = jnp.minimum(source_of - 1, most - sink)
    moved = jax.random.randint(jax.random.fold_in(stream_key, 1), (couples,), 0, 1 << 20) % (room + 1)
    tallies = tallies.at[1:1 + 2 * couples:2].set(source_of - moved).at[2:2 + 2 * couples:2].set(sink + moved)
    return tallies[jax.random.permutation(jax.random.fold_in(stream_key, 2), amount)]


def normal_values(stream_key, extent, width, reach, pieces=(), kind=jnp.bfloat16):
    entries = jax.random.normal(stream_key, extent, jnp.float32) * width
    if len(pieces) > 0:
        entries = block_scale(stream_key, extent, pieces, -0.22, 0.18) * entries
    return jnp.clip(entries, min=-reach, max=reach).astype(kind)


def noise_with(key, shape, width, most, cuts, heavy, kind=jnp.bfloat16):
    values = width * jax.random.normal(key, shape, jnp.float32)
    if cuts:
        values = values * block_scale(key, shape, cuts, -0.22, 0.18)
    return jnp.clip(with_spikes(values, jax.random.fold_in(key, 3), *heavy), -most, most).astype(kind)


def setup_inputs(seed: int = 0) -> dict:
    key_list = jax.random.split(jax.random.key(seed), 10)
    return {
        "hyena_query": normal_values(key_list[0], (LENGTH, D), 1.0, 6.0, ((0, 8), (1, 16))),
        "hyena_key": normal_values(key_list[1], (LENGTH, D), 1.0, 6.0, ((0, 8), (1, 16))),
        "hyena_value": normal_values(key_list[2], (LENGTH, D), 1.0, 6.0, ((0, 8), (1, 16))),
        "hyena_filter": normal_values(key_list[3], (FILT, D), FILT ** -0.5, 0.5, ((1, 16),)),
        "attn_query": draw_attn_query(jax.random.fold_in(key_list[9], 71), 0),
        "attn_key": draw_attn_key(jax.random.fold_in(key_list[9], 71), 0),
        "attn_value": normal_values(key_list[6], (LENGTH, D), 2.0, 12.0, ((0, 8), (1, 16))),
        "segment_ids": jnp.searchsorted(jnp.cumsum(ragged_sizes(key_list[7], SEGS, LENGTH, LENGTH // 2, 0)), jnp.arange(LENGTH), side="right").astype(jnp.int32),
        "out_weight": noise_with(key_list[8], (D, D), D ** -0.5, 0.09375, ((0, 16),), (0, 1, 16, 2.0)),
    }


def hyena_mix(hyena_query, hyena_key, hyena_value, hyena_filter):
    signal = lax.optimization_barrier((hyena_key.astype(jnp.float32) * hyena_value.astype(jnp.float32)).astype(jnp.bfloat16)).astype(jnp.float32)
    padded = jnp.pad(signal, ((FILT, 0), (0, 0)))
    filter_taps = hyena_filter.astype(jnp.float32)

    def add_tap(tap_index, filtered):
        tap_row = lax.dynamic_index_in_dim(filter_taps, tap_index, 0, keepdims=True)
        moved = lax.dynamic_slice_in_dim(padded, (FILT - tap_index).astype(jnp.int32), LENGTH, 0)
        return filtered + tap_row * moved

    filtered = lax.fori_loop(jnp.int32(0), jnp.int32(FILT), add_tap, jnp.zeros((LENGTH, D), jnp.float32))
    return (hyena_query.astype(jnp.float32) * filtered).astype(jnp.bfloat16)


def reference(hyena_query, hyena_key, hyena_value, hyena_filter, attn_query, attn_key, attn_value, segment_ids, out_weight):
    hyena_out = hyena_mix(hyena_query, hyena_key, hyena_value, hyena_filter)
    positions = jnp.arange(LENGTH, dtype=jnp.int32)
    allowed = (positions[None, :] <= positions[:, None]) & (segment_ids[None, :] == segment_ids[:, None])
    score_scale = HEAD_DIM ** -0.5

    def one_head(head_index):
        first_col = (head_index * HEAD_DIM).astype(jnp.int32)
        query_head = lax.dynamic_slice_in_dim(attn_query, first_col, HEAD_DIM, 1)
        key_head = lax.dynamic_slice_in_dim(attn_key, first_col, HEAD_DIM, 1)
        value_head = lax.dynamic_slice_in_dim(attn_value, first_col, HEAD_DIM, 1)
        scores = jnp.dot(query_head, key_head.T, preferred_element_type=jnp.float32) * score_scale
        row_top = jnp.max(jnp.where(allowed, scores, -1e30), axis=1)
        probs = jnp.where(allowed, jnp.exp(scores - row_top[:, None]), 0.0)
        row_total = jnp.sum(probs, axis=1)
        weighted = jnp.dot(probs.astype(jnp.bfloat16), value_head, preferred_element_type=jnp.float32)
        return (weighted / row_total[:, None]).astype(jnp.bfloat16)

    head_outputs = lax.map(one_head, jnp.arange(HEADS, dtype=jnp.int32))
    attended = jnp.transpose(head_outputs, (1, 0, 2)).reshape(LENGTH, D)
    group_width = D // N_HEAD

    def add_group(group_index, total):
        first_col = (group_index * group_width).astype(jnp.int32)
        columns = lax.dynamic_slice_in_dim(attended, first_col, group_width, 1)
        rows = lax.dynamic_slice_in_dim(out_weight, first_col, group_width, 0)
        term = jnp.dot(columns, rows, preferred_element_type=jnp.float32).astype(jnp.bfloat16)
        return total + term.astype(jnp.float32)

    projected = lax.fori_loop(jnp.int32(0), jnp.int32(N_HEAD), add_group, jnp.zeros((LENGTH, D), jnp.float32))
    stream = (hyena_out.astype(jnp.float32) + projected).astype(jnp.bfloat16)
    return (hyena_out, stream)
```

```python
import functools
import math

import jax
import jax.numpy as jnp
from jax import lax
from jax.experimental import pallas as pl
from jax.experimental.pallas import tpu as pltpu
from jax.sharding import PartitionSpec as P

HEAD_DIM = 128
ROWS = 512
HALF = 2048
BK = 512
SCALE = HEAD_DIM ** -0.5
LOG2E = math.log2(math.e)
F32 = jnp.float32
BF16 = jnp.bfloat16
VMEM_LIMIT = 56 * 1024 * 1024


def z_pairs(by):
    return [(i, (i // 4) * 4 + (i % 4 + by) % 4) for i in range(8)]


def cross_pairs(by):
    return [(i, 4 + (i + by) % 4) for i in range(4)]


def y_pairs(by):
    return [(i, ((i // 4 + by) % 4) * 4 + i % 4) for i in range(16)]


def flip_pairs(mask):
    return [(i, i ^ mask) for i in range(16)]


def vmem_specs(count):
    return [pl.BlockSpec(memory_space=pltpu.VMEM)] * count


def pack_kernel(place, q_ref, k_ref, v_ref, *outs):
    z = place[0]
    for by in range(4):
        cols = pl.ds(pl.multiple_of(lax.rem(z + by, 4) * 128, 128), 128)
        qkv, kv = outs[by], outs[4 + by]
        qkv[:, 0:128] = q_ref[:, cols]
        key = k_ref[:, cols]
        val = v_ref[:, cols]
        qkv[:, 128:256] = key
        qkv[:, 256:384] = val
        kv[:, 0:128] = key
        kv[:, 128:256] = val


def pack(place, q, k, v):
    outs = [jax.ShapeDtypeStruct((ROWS, 384), BF16)] * 4 + [jax.ShapeDtypeStruct((ROWS, 256), BF16)] * 4
    return pl.pallas_call(
        pack_kernel,
        grid_spec=pltpu.PrefetchScalarGridSpec(
            num_scalar_prefetch=1, grid=(), in_specs=vmem_specs(3), out_specs=vmem_specs(8)
        ),
        out_shape=outs,
        name="pack",
        compiler_params=pltpu.CompilerParams(vmem_limit_bytes=VMEM_LIMIT),
        cost_estimate=pl.CostEstimate(flops=0, bytes_accessed=4 * 1024 * 1024, transcendentals=0),
    )(place, q, k, v)


def attention_kernel(place, low, start_ref, *refs):
    own = refs[0:4]
    cross = refs[4:8]
    outs = refs[8:12]
    q_s, k_s, v_s, m_s, l_s, acc_s = refs[12:]
    z = place[0]
    shift = place[1]
    for by in range(4):
        row = pl.multiple_of(lax.rem(z + 4 - by, 4) * ROWS, ROWS)
        q_s[pl.ds(row, ROWS), :] = own[by][:, 0:128]
        k_s[pl.ds(HALF + row, ROWS), :] = own[by][:, 128:256]
        v_s[pl.ds(HALF + row, ROWS), :] = own[by][:, 256:384]
        k_s[pl.ds(row, ROWS), :] = cross[by][:, 0:128]
        v_s[pl.ds(row, ROWS), :] = cross[by][:, 128:256]
    key_iota = lax.broadcasted_iota(jnp.int32, (BK, ROWS), 0)
    diff_iota = key_iota - lax.broadcasted_iota(jnp.int32, (BK, ROWS), 1)

    def step(block, query, first, bound, diagonal):
        row = pl.multiple_of(block * BK, BK)
        key = k_s[pl.ds(row, BK), :]
        val = v_s[pl.ds(row, BK), :]
        scores = lax.dot_general(key, query, (((1,), (1,)), ((), ())), preferred_element_type=F32)
        allowed = key_iota >= bound - row
        if diagonal:
            allowed = allowed & (diff_iota <= 0)
        scores = jnp.where(allowed, scores, -1e30)
        top = jnp.max(scores, axis=0, keepdims=True)
        if not first:
            old = m_s[0:1, :]
            top = jnp.maximum(old, top)
        probs = jnp.exp2((scores - top) * (SCALE * LOG2E))
        total = jnp.sum(probs, axis=0, keepdims=True)
        out = lax.dot_general(val, probs.astype(BF16), (((0,), (0,)), ((), ())), preferred_element_type=F32)
        if not first:
            factor = jnp.exp2((old - top) * (SCALE * LOG2E))
            total = total + l_s[0:1, :] * factor
            out = out + acc_s[...] * factor
        m_s[0:1, :] = top
        l_s[0:1, :] = total
        acc_s[...] = out

    for by in range(4):
        block = lax.rem(z + by, 4)
        query = q_s[pl.ds(pl.multiple_of(block * ROWS, ROWS), ROWS), :]
        bound = start_ref[pl.ds(block, 1), :] + shift
        step(4 + block, query, True, bound, True)

        def body(i, carry, block=block, query=query, bound=bound):
            step(3 + block - i, query, False, bound, False)
            return carry

        lax.fori_loop(0, 4 + block - low[block], body, 0)
        outs[by][...] = jnp.transpose(acc_s[...] / l_s[0:1, :]).astype(BF16)


def attention(place, low, starts, own, cross):
    return pl.pallas_call(
        attention_kernel,
        grid_spec=pltpu.PrefetchScalarGridSpec(
            num_scalar_prefetch=2,
            grid=(),
            in_specs=vmem_specs(9),
            out_specs=vmem_specs(4),
            scratch_shapes=[
                pltpu.VMEM((HALF, 128), BF16),
                pltpu.VMEM((2 * HALF, 128), BF16),
                pltpu.VMEM((2 * HALF, 128), BF16),
                pltpu.VMEM((8, ROWS), F32),
                pltpu.VMEM((8, ROWS), F32),
                pltpu.VMEM((128, ROWS), F32),
            ],
        ),
        out_shape=[jax.ShapeDtypeStruct((ROWS, 128), BF16)] * 4,
        name="attention",
        compiler_params=pltpu.CompilerParams(vmem_limit_bytes=VMEM_LIMIT),
        cost_estimate=pl.CostEstimate(flops=4 * 10**9, bytes_accessed=4 * 1024 * 1024, transcendentals=4 * 10**6),
    )(place, low, starts, *own, *cross)


def project_kernel(groups, half, place, own_ref, sib_ref, w_own, w_sib, *rest):
    outs = rest[:-1]
    att = rest[-1]
    j = pl.program_id(0)
    rows = ROWS // 2

    @pl.when(j == 0)
    def _():
        z = place[0]
        for by in range(4):
            col = pl.multiple_of(lax.rem(z + 4 - by, 4) * 128, 128)
            first = by * ROWS + half * rows
            att[:, pl.ds(col, 128)] = own_ref[first : first + rows, :]
            att[:, pl.ds(512 + col, 128)] = sib_ref[first : first + rows, :]

    term = jnp.dot(att[:, 0:512], w_own[...], preferred_element_type=F32)
    term = term + jnp.dot(att[:, 512:1024], w_sib[...], preferred_element_type=F32)
    term = term.astype(BF16)
    first = 0
    for out, group in zip(outs, groups):
        @pl.when((j >= first) & (j < first + len(group)))
        def _(out=out):
            out[0] = term

        first += len(group)


def project(groups, half, place, own, sib, w_own, w_sib):
    flat = [item for group in groups for item in group]
    steps = len(flat)
    rows = ROWS // 2

    def pick(j, which):
        value = jnp.int32(flat[0][which])
        for i in range(1, steps):
            value = jnp.where(j == i, jnp.int32(flat[i][which]), value)
        return value

    def column(j, place):
        y = lax.rem(place[2] + pick(j, 0), 4)
        x = lax.rem(place[3] + pick(j, 1), 2)
        return y * 2 + x

    out_specs = []
    out_shape = []
    first = 0
    for group in groups:
        out_specs.append(
            pl.BlockSpec(
                (1, rows, 512),
                lambda j, place, first=first, last=len(group) - 1: (jnp.clip(j - first, 0, last), 0, 0),
            )
        )
        out_shape.append(jax.ShapeDtypeStruct((len(group), rows, 512), BF16))
        first += len(group)
    return pl.pallas_call(
        functools.partial(project_kernel, groups, half),
        grid_spec=pltpu.PrefetchScalarGridSpec(
            num_scalar_prefetch=1,
            grid=(steps,),
            in_specs=[
                pl.BlockSpec((4 * ROWS, 128), lambda j, place: (0, 0)),
                pl.BlockSpec((4 * ROWS, 128), lambda j, place: (0, 0)),
                pl.BlockSpec((512, 512), lambda j, place: (0, column(j, place) * 2 + place[4])),
                pl.BlockSpec((512, 512), lambda j, place: (0, column(j, place))),
            ],
            out_specs=out_specs,
            scratch_shapes=[pltpu.VMEM((rows, 1024), BF16)],
        ),
        out_shape=out_shape,
        name="project",
        compiler_params=pltpu.CompilerParams(vmem_limit_bytes=VMEM_LIMIT),
        cost_estimate=pl.CostEstimate(
            flops=steps * 2 * rows * 1024 * 512, bytes_accessed=steps * 1024 * 1300 + 1024 * 1024, transcendentals=0
        ),
    )(place, own, sib, w_own, w_sib)


def hyena_kernel(q_ref, k_ref, v_ref, rim_ref, f_ref, out_ref, sig, shifted, taps):
    for lane in range(4):
        cols = slice(lane * 128, lane * 128 + 128)
        sig[0:128, :] = rim_ref[:, cols].astype(F32)
        product = k_ref[:, cols].astype(F32) * v_ref[:, cols].astype(F32)
        sig[128:640, :] = product.astype(BF16).astype(F32)
        taps[...] = f_ref[:, cols].astype(F32)
        for by in range(8):
            shifted[by, 8:640, :] = sig[8 - by : 640 - by, :]

        def block(b, carry):
            base = 128 + b * 128

            def one_shift(by, acc):
                for high in range(16):
                    tap = taps[pl.ds(high * 8 + by, 1), :]
                    acc = acc + tap * shifted[by, pl.ds(pl.multiple_of(base - high * 8, 8), 128), :]
                return acc

            acc = lax.fori_loop(0, 8, one_shift, jnp.zeros((128, 128), F32))
            rows = pl.ds(pl.multiple_of(b * 128, 128), 128)
            out_ref[rows, cols] = (q_ref[rows, cols].astype(F32) * acc).astype(BF16)
            return carry

        lax.fori_loop(0, 4, block, 0)


def hyena(q, k, v, rim, taps):
    return pl.pallas_call(
        hyena_kernel,
        in_specs=vmem_specs(5),
        out_specs=pl.BlockSpec(memory_space=pltpu.VMEM),
        scratch_shapes=[
            pltpu.VMEM((640, 128), F32),
            pltpu.VMEM((8, 640, 128), F32),
            pltpu.VMEM((128, 128), F32),
        ],
        out_shape=jax.ShapeDtypeStruct((ROWS, 512), BF16),
        name="hyena",
        compiler_params=pltpu.CompilerParams(vmem_limit_bytes=VMEM_LIMIT),
        cost_estimate=pl.CostEstimate(flops=10**10, bytes_accessed=3 * 1024 * 1024, transcendentals=0),
    )(q, k, v, rim, taps)


def on_device(
    hyena_query,
    hyena_key,
    hyena_value,
    hyena_filter,
    attn_query,
    attn_key,
    attn_value,
    segment_ids,
    out_weight,
):
    ctx = lax.axis_index("ctx")
    head = lax.axis_index("head")
    z = ctx % 4
    x_hi = ctx // 4
    core = head % 2
    shift = HALF - x_hi * HALF
    place = jnp.stack([z, shift, head // 4, (head // 2) % 2, core]).astype(jnp.int32)

    packed = pack(place, attn_query, attn_key, attn_value)
    own = [packed[0]] + [lax.ppermute(packed[by], "ctx", z_pairs(by)) for by in (1, 2, 3)]
    cross = [lax.ppermute(packed[4 + by], "ctx", cross_pairs(by)) for by in range(4)]

    weight_view = out_weight.reshape(512, 8, 2, 512)
    to_sibling = lax.dynamic_index_in_dim(weight_view, 1 - core, 2, keepdims=False).reshape(512, 4096)
    w_sib = lax.ppermute(to_sibling, "head", flip_pairs(1))

    edge = (hyena_key[384:].astype(F32) * hyena_value[384:].astype(F32)).astype(BF16)
    rim = lax.ppermute(edge, "ctx", [(i, i + 1) for i in range(7)])
    hyena_out = hyena(hyena_query, hyena_key, hyena_value, rim, hyena_filter)

    my_ids = lax.dynamic_slice_in_dim(segment_ids, x_hi * HALF, HALF)
    starts = jnp.zeros((HALF,), jnp.int32)
    for value in range(5):
        count = jnp.sum((segment_ids == value).astype(jnp.int32))
        starts = starts + jnp.where(my_ids > value, count, 0)
    starts = starts.reshape(4, ROWS)
    low = (starts[:, 0] + shift) // BK
    attended = attention(place, low, starts, own, cross)
    mine = jnp.concatenate(
        [attended[0]] + [lax.ppermute(attended[by], "ctx", z_pairs(by)) for by in (1, 2, 3)], axis=0
    )
    sib = lax.ppermute(mine, "head", flip_pairs(1))

    (b_send,) = project([[(d, 1) for d in range(4)]], 1, place, mine, sib, out_weight, w_sib)
    b_got = lax.ppermute(b_send, "head", flip_pairs(2))
    a_send = project([[(d, 0), (d, 1)] for d in (1, 2, 3)], 0, place, mine, sib, out_weight, w_sib)
    a_got = [lax.ppermute(a_send[d - 1], "head", y_pairs(d)) for d in (1, 2, 3)]
    (b_keep,) = project([[(d, 0) for d in range(4)]], 1, place, mine, sib, out_weight, w_sib)
    (a_keep,) = project([[(0, 0), (0, 1)]], 0, place, mine, sib, out_weight, w_sib)

    b_sum = b_keep.astype(F32) + b_got.astype(F32)
    b_parts = [b_sum[d].astype(BF16) for d in range(4)]
    b_terms = [lax.ppermute(b_parts[d], "head", y_pairs(d)) for d in (1, 2, 3)]

    def a_total(e):
        total = a_keep[e].astype(F32)
        for got in a_got:
            total = total + got[e].astype(F32)
        return total

    a_term = lax.ppermute(a_total(1).astype(BF16), "head", flip_pairs(2))
    a_final = a_total(0) + a_term.astype(F32)
    b_final = b_sum[0]
    for term in b_terms:
        b_final = b_final + term.astype(F32)
    stream_a = (hyena_out[:256].astype(F32) + a_final).astype(BF16)
    stream_b = (hyena_out[256:].astype(F32) + b_final).astype(BF16)
    stream = jnp.concatenate([stream_a, stream_b], axis=0)
    return (hyena_out, stream)


def solution(mesh):
    return jax.shard_map(
        on_device,
        mesh=mesh,
        in_specs=(
            P("ctx", "head"),
            P("ctx", "head"),
            P("ctx", "head"),
            P(None, "head"),
            P("ctx", "head"),
            P("ctx", "head"),
            P("ctx", "head"),
            P(),
            P("head", None),
        ),
        out_specs=(P("ctx", "head"), P("ctx", "head")),
        check_vma=False,
    )
```

```python
import functools
import math

import jax
import jax.numpy as jnp
from jax import lax
from jax.experimental import pallas as pl
from jax.experimental.pallas import tpu as pltpu
from jax.sharding import PartitionSpec as P

HEAD_DIM = 128
ROWS = 512
HALF = 2048
BK = 512
SCALE = HEAD_DIM ** -0.5
LOG2E = math.log2(math.e)
F32 = jnp.float32
BF16 = jnp.bfloat16
MIB = 1024 * 1024


def z_pairs(by):
    return [(i, (i // 4) * 4 + (i % 4 + by) % 4) for i in range(8)]


def cross_pairs(by):
    return [(i, 4 + (i + by) % 4) for i in range(4)]


def y_pairs(by):
    return [(i, ((i // 4 + by) % 4) * 4 + i % 4) for i in range(16)]


def flip_pairs(mask):
    return [(i, i ^ mask) for i in range(16)]


def vmem_specs(count):
    return [pl.BlockSpec(memory_space=pltpu.VMEM)] * count


def pack_kernel(q_ref, k_ref, v_ref, out_ref):
    for to in range(4):
        for i, ref in enumerate((q_ref, k_ref, v_ref)):
            out_ref[to, :, i * 128 : i * 128 + 128] = ref[:, to * 128 : to * 128 + 128]


def pack(q, k, v):
    return pl.pallas_call(
        pack_kernel,
        in_specs=vmem_specs(3),
        out_specs=pl.BlockSpec(memory_space=pltpu.VMEM),
        out_shape=jax.ShapeDtypeStruct((4, ROWS, 384), BF16),
        name="pack",
        compiler_params=pltpu.CompilerParams(vmem_limit_bytes=60 * MIB),
        cost_estimate=pl.CostEstimate(flops=0, bytes_accessed=3 * MIB, transcendentals=0),
    )(q, k, v)


def pack_cross_kernel(place, k_ref, v_ref, *outs):
    for by in range(4):
        cols = pl.ds(pl.multiple_of(lax.rem(place[0] + by, 4) * 128, 128), 128)
        outs[by][:, 0:128] = k_ref[:, cols]
        outs[by][:, 128:256] = v_ref[:, cols]


def pack_cross(place, k, v):
    return pl.pallas_call(
        pack_cross_kernel,
        grid_spec=pltpu.PrefetchScalarGridSpec(
            num_scalar_prefetch=1, grid=(), in_specs=vmem_specs(2), out_specs=vmem_specs(4)
        ),
        out_shape=[jax.ShapeDtypeStruct((ROWS, 256), BF16)] * 4,
        name="pack_cross",
        compiler_params=pltpu.CompilerParams(vmem_limit_bytes=60 * MIB),
        cost_estimate=pl.CostEstimate(flops=0, bytes_accessed=2 * MIB, transcendentals=0),
    )(place, k, v)


def attention_kernel(order, place, ids_ref, *refs):
    own = refs[0]
    cross = refs[1:5]
    outs = refs[5 : 5 + len(order)]
    q_s, k_s, v_s, bound_s, m_s, l_s, acc_s = refs[5 + len(order) :]
    z = place[0]
    shift = place[1]
    for by in range(4):
        row = pl.multiple_of(lax.rem(z + 4 - by, 4) * ROWS, ROWS)
        at = by * ROWS
        q_s[at : at + ROWS, :] = own[by, :, 0:128]
        k_s[HALF + at : HALF + at + ROWS, :] = own[by, :, 128:256]
        v_s[HALF + at : HALF + at + ROWS, :] = own[by, :, 256:384]
        k_s[pl.ds(row, ROWS), :] = cross[by][:, 0:128]
        v_s[pl.ds(row, ROWS), :] = cross[by][:, 128:256]
    ids = ids_ref[...]
    bounds = jnp.full(ids.shape, shift, jnp.int32)
    for value in range(5):
        count = jnp.sum(jnp.where(ids == value, 1.0, 0.0)).astype(jnp.int32)
        bounds = bounds + jnp.where(ids > value, count, 0)
    bound_s[...] = bounds
    key_iota = lax.broadcasted_iota(jnp.int32, (BK, ROWS), 0)
    diff_iota = key_iota - lax.broadcasted_iota(jnp.int32, (BK, ROWS), 1)

    def step(block, query, first, bound, diagonal):
        row = pl.multiple_of(block * BK, BK)
        key = k_s[pl.ds(row, BK), :]
        val = v_s[pl.ds(row, BK), :]
        scores = lax.dot_general(key, query, (((1,), (1,)), ((), ())), preferred_element_type=F32)
        allowed = key_iota >= bound - row
        if diagonal:
            allowed = allowed & (diff_iota <= 0)
        scores = jnp.where(allowed, scores, -1e30)
        top = jnp.max(scores, axis=0, keepdims=True)
        if not first:
            old = m_s[0:1, :]
            top = jnp.maximum(old, top)
        probs = jnp.exp2((scores - top) * (SCALE * LOG2E))
        total = jnp.sum(probs, axis=0, keepdims=True)
        out = lax.dot_general(val, probs.astype(BF16), (((0,), (0,)), ((), ())), preferred_element_type=F32)
        if not first:
            factor = jnp.exp2((old - top) * (SCALE * LOG2E))
            total = total + l_s[0:1, :] * factor
            out = out + acc_s[...] * factor
        m_s[0:1, :] = top
        l_s[0:1, :] = total
        acc_s[...] = out

    for out, by in zip(outs, order):
        block = lax.rem(z + by, 4)
        query = q_s[pl.ds(pl.multiple_of(block * ROWS, ROWS), ROWS), :]
        bound = bound_s[pl.ds(place[5] + block, 1), :]
        low = jnp.min(bound) // BK
        step(4 + block, query, True, bound, True)

        def body(i, carry, block=block, query=query, bound=bound):
            step(3 + block - i, query, False, bound, False)
            return carry

        lax.fori_loop(0, 4 + block - low, body, 0)
        out[...] = jnp.transpose(acc_s[...] / l_s[0:1, :]).astype(BF16)


def attention(order, place, ids, own, cross):
    return pl.pallas_call(
        functools.partial(attention_kernel, order),
        grid_spec=pltpu.PrefetchScalarGridSpec(
            num_scalar_prefetch=1,
            grid=(),
            in_specs=vmem_specs(6),
            out_specs=vmem_specs(len(order)),
            scratch_shapes=[
                pltpu.VMEM((HALF, 128), BF16),
                pltpu.VMEM((2 * HALF, 128), BF16),
                pltpu.VMEM((2 * HALF, 128), BF16),
                pltpu.VMEM((8, ROWS), jnp.int32),
                pltpu.VMEM((8, ROWS), F32),
                pltpu.VMEM((8, ROWS), F32),
                pltpu.VMEM((128, ROWS), F32),
            ],
        ),
        out_shape=[jax.ShapeDtypeStruct((ROWS, 128), BF16)] * len(order),
        name="attention",
        compiler_params=pltpu.CompilerParams(vmem_limit_bytes=20 * MIB),
        cost_estimate=pl.CostEstimate(
            flops=len(order) * 10**9, bytes_accessed=4 * MIB, transcendentals=len(order) * 10**6
        ),
    )(place, ids, own, *cross)


BLOCKS = [(0, 1), (1, 1), (2, 1), (3, 1), (2, 0), (1, 0), (3, 0), (0, 0)]


def project_kernel(place, own_ref, sib_ref, w_own, w_sib, *rest):
    a_refs, b_refs = rest[:4], rest[4:6]
    att, weights, staged, in_sem, out_sem = rest[6:]
    z = place[0]
    copies = []
    for j, (d, e) in enumerate(BLOCKS):
        block = (lax.rem(place[2] + d, 4) * 2 + lax.rem(place[3] + e, 2)) * 2 + place[4]
        cols = pl.ds(pl.multiple_of(block * 512, 512), 512)
        pair = []
        for i, ref in enumerate((w_own, w_sib)):
            pair.append(pltpu.make_async_copy(ref.at[:, cols], weights.at[j, pl.ds(i * 512, 512), :], in_sem.at[j, i]))
            pair[-1].start()
        copies.append(pair)
    for by in range(4):
        col = pl.multiple_of(lax.rem(z + 4 - by, 4) * 128, 128)
        first = by * ROWS
        att[:, pl.ds(col, 128)] = own_ref[first : first + ROWS, :]
        att[:, pl.ds(512 + col, 128)] = sib_ref[first : first + ROWS, :]
    stores = []
    for j, (d, e) in enumerate(BLOCKS):
        for copy in copies[j]:
            copy.wait()
        staged[j] = jnp.dot(att[...], weights[j], preferred_element_type=F32).astype(BF16)
        stores.append(pltpu.make_async_copy(staged.at[j, pl.ds(0, 256), :], a_refs[d].at[e], out_sem.at[j, 0]))
        stores.append(pltpu.make_async_copy(staged.at[j, pl.ds(256, 256), :], b_refs[e].at[d], out_sem.at[j, 1]))
        stores[-2].start()
        stores[-1].start()
    for copy in stores:
        copy.wait()


def project(place, own, sib, w_own, w_sib):
    anywhere = pl.BlockSpec(memory_space=pl.ANY)
    return pl.pallas_call(
        project_kernel,
        grid_spec=pltpu.PrefetchScalarGridSpec(
            num_scalar_prefetch=1,
            grid=(),
            in_specs=vmem_specs(2) + [anywhere] * 2,
            out_specs=[anywhere] * 6,
            scratch_shapes=[
                pltpu.VMEM((ROWS, 1024), BF16),
                pltpu.VMEM((8, 1024, 512), BF16),
                pltpu.VMEM((8, ROWS, 512), BF16),
                pltpu.SemaphoreType.DMA((8, 2)),
                pltpu.SemaphoreType.DMA((8, 2)),
            ],
        ),
        out_shape=[jax.ShapeDtypeStruct((2, 256, 512), BF16)] * 4 + [jax.ShapeDtypeStruct((4, 256, 512), BF16)] * 2,
        name="project",
        compiler_params=pltpu.CompilerParams(vmem_limit_bytes=56 * MIB),
        cost_estimate=pl.CostEstimate(flops=8 * 2 * ROWS * 1024 * 512, bytes_accessed=14 * MIB, transcendentals=0),
    )(place, own, sib, w_own, w_sib)


def hyena_kernel(q_ref, k_ref, v_ref, rim_ref, f_ref, out_ref, sig, shifted, taps):
    for lane in range(4):
        cols = slice(lane * 128, lane * 128 + 128)
        sig[0:128, :] = rim_ref[:, cols].astype(F32)
        product = k_ref[:, cols].astype(F32) * v_ref[:, cols].astype(F32)
        sig[128:640, :] = product.astype(BF16).astype(F32)
        taps[...] = f_ref[:, cols].astype(F32)
        for by in range(8):
            shifted[by, 8:640, :] = sig[8 - by : 640 - by, :]

        def block(b, carry):
            base = 128 + b * 128

            def one_shift(by, acc):
                for high in range(16):
                    tap = taps[pl.ds(high * 8 + by, 1), :]
                    acc = acc + tap * shifted[by, pl.ds(pl.multiple_of(base - high * 8, 8), 128), :]
                return acc

            acc = lax.fori_loop(0, 8, one_shift, jnp.zeros((128, 128), F32))
            rows = pl.ds(pl.multiple_of(b * 128, 128), 128)
            out_ref[rows, cols] = (q_ref[rows, cols].astype(F32) * acc).astype(BF16)
            return carry

        lax.fori_loop(0, 4, block, 0)


def hyena(q, k, v, rim, taps):
    return pl.pallas_call(
        hyena_kernel,
        in_specs=vmem_specs(5),
        out_specs=pl.BlockSpec(memory_space=pltpu.VMEM),
        scratch_shapes=[
            pltpu.VMEM((640, 128), F32),
            pltpu.VMEM((8, 640, 128), F32),
            pltpu.VMEM((128, 128), F32),
        ],
        out_shape=jax.ShapeDtypeStruct((ROWS, 512), BF16),
        name="hyena",
        compiler_params=pltpu.CompilerParams(vmem_limit_bytes=12 * MIB),
        cost_estimate=pl.CostEstimate(flops=10**7, bytes_accessed=3 * 1024, transcendentals=0),
    )(q, k, v, rim, taps)


def on_device(
    hyena_query,
    hyena_key,
    hyena_value,
    hyena_filter,
    attn_query,
    attn_key,
    attn_value,
    segment_ids,
    out_weight,
):
    ctx = lax.axis_index("ctx")
    head = lax.axis_index("head")
    z = ctx % 4
    x_hi = ctx // 4
    core = head % 2
    shift = HALF - x_hi * HALF
    place = jnp.stack([z, shift, head // 4, (head // 2) % 2, core, x_hi * 4]).astype(jnp.int32)

    w_sib = lax.ppermute(out_weight, "head", flip_pairs(1))
    to_cross = pack_cross(place, attn_key, attn_value)
    query, _ = lax.optimization_barrier((attn_query, to_cross[0]))
    packed = pack(query, attn_key, attn_value)
    cross = [lax.ppermute(to_cross[by], "ctx", cross_pairs(by)) for by in range(4)]
    own = lax.all_to_all(packed, "ctx", 0, 0, axis_index_groups=[[0, 1, 2, 3], [4, 5, 6, 7]])

    late_key, late_value, _ = lax.optimization_barrier((hyena_key[384:], hyena_value[384:], w_sib))
    edge = (late_key.astype(F32) * late_value.astype(F32)).astype(BF16)
    rim = lax.ppermute(edge, "ctx", [(i, i + 1) for i in range(7)])
    own, rim = lax.optimization_barrier((own, rim))

    ids = segment_ids.reshape(8, ROWS)
    attended = attention((2, 1, 3), place, ids, own, cross)
    back = [lax.ppermute(part, "ctx", z_pairs(by)) for part, by in zip(attended, (2, 1, 3))]
    (kept,) = attention((0,), place, ids, own, cross)
    mine = jnp.concatenate([kept, back[1], back[0], back[2]], axis=0)
    sib = lax.ppermute(mine, "head", flip_pairs(1))

    *a_terms, b_keep, b_send = project(place, mine, sib, out_weight, w_sib)
    a_keep = a_terms[0]
    b_got = lax.ppermute(b_send, "head", flip_pairs(2))
    a_got = [lax.ppermute(a_terms[d], "head", y_pairs(d)) for d in (2, 1, 3)]
    rim, _ = lax.optimization_barrier((rim, b_keep))
    hyena_out = hyena(hyena_query, hyena_key, hyena_value, rim, hyena_filter)
    hyena_out, b_got = lax.optimization_barrier((hyena_out, b_got))

    b_sum = b_keep.astype(F32) + b_got.astype(F32)
    b_parts = [b_sum[d].astype(BF16) for d in range(4)]
    a_got, _ = lax.optimization_barrier((a_got, b_parts))
    b_terms = [lax.ppermute(b_parts[d], "head", y_pairs(d)) for d in (1, 2, 3)]

    def a_total(e):
        total = a_keep[e].astype(F32)
        for got in a_got:
            total = total + got[e].astype(F32)
        return total

    a_term = lax.ppermute(a_total(1).astype(BF16), "head", flip_pairs(2))
    a_final = a_total(0) + a_term.astype(F32)
    b_final = b_sum[0]
    for term in b_terms:
        b_final = b_final + term.astype(F32)
    stream_a = (hyena_out[:256].astype(F32) + a_final).astype(BF16)
    stream_b = (hyena_out[256:].astype(F32) + b_final).astype(BF16)
    stream = jnp.concatenate([stream_a, stream_b], axis=0)
    return (hyena_out, stream)


def solution(mesh):
    return jax.shard_map(
        on_device,
        mesh=mesh,
        in_specs=(
            P("ctx", "head"),
            P("ctx", "head"),
            P("ctx", "head"),
            P(None, "head"),
            P("ctx", "head"),
            P("ctx", "head"),
            P("ctx", "head"),
            P(),
            P("head", None),
        ),
        out_specs=(P("ctx", "head"), P("ctx", "head")),
        check_vma=False,
    )
```

```python
import functools
import math

import jax
import jax.numpy as jnp
from jax import lax
from jax.experimental import pallas as pl
from jax.experimental.pallas import tpu as pltpu
from jax.sharding import PartitionSpec as P

HEAD_DIM = 128
ROWS = 512
A_ROWS = 288
B_ROWS = ROWS - A_ROWS
HALF = 2048
BK = 512
SCALE = HEAD_DIM ** -0.5
LOG2E = math.log2(math.e)
F32 = jnp.float32
BF16 = jnp.bfloat16
MIB = 1024 * 1024


def z_pairs(by):
    return [(i, (i // 4) * 4 + (i % 4 + by) % 4) for i in range(8)]


def cross_pairs(by):
    return [(i, 4 + (i + by) % 4) for i in range(4)]


def y_pairs(by):
    return [(i, ((i // 4 + by) % 4) * 4 + i % 4) for i in range(16)]


def flip_pairs(mask):
    return [(i, i ^ mask) for i in range(16)]


def vmem_specs(count):
    return [pl.BlockSpec(memory_space=pltpu.VMEM)] * count


DIRECT = (0, 1, 3)


def pack_kernel(q_ref, k_ref, v_ref, all_ref, *outs):
    for to in range(4):
        for i, ref in enumerate((q_ref, k_ref, v_ref)):
            all_ref[to, :, i * 128 : i * 128 + 128] = ref[:, to * 128 : to * 128 + 128]
    z = lax.rem(lax.axis_index("ctx"), 4)
    for out, by in zip(outs, DIRECT):
        cols = pl.ds(pl.multiple_of(lax.rem(z + by, 4) * 128, 128), 128)
        out[:, 0:128] = k_ref[:, cols]
        out[:, 128:256] = v_ref[:, cols]


def pack(q, k, v):
    return pl.pallas_call(
        pack_kernel,
        in_specs=vmem_specs(3),
        out_specs=vmem_specs(4),
        out_shape=[jax.ShapeDtypeStruct((4, ROWS, 384), BF16)] + [jax.ShapeDtypeStruct((ROWS, 256), BF16)] * 3,
        name="pack",
        compiler_params=pltpu.CompilerParams(vmem_limit_bytes=60 * MIB),
        cost_estimate=pl.CostEstimate(flops=0, bytes_accessed=4 * MIB, transcendentals=0),
    )(q, k, v)


def document_starts(ids):
    starts = jnp.zeros(ids.shape, jnp.int32)
    for value in range(5):
        count = jnp.sum(jnp.where(ids == value, 1.0, 0.0)).astype(jnp.int32)
        starts = starts + jnp.where(ids > value, count, 0)
    return starts


def softmax_step(query, key, val, allowed, before):
    scores = lax.dot_general(key, query, (((1,), (1,)), ((), ())), preferred_element_type=F32)
    scores = jnp.where(allowed, scores, -1e30)
    top = jnp.max(scores, axis=0, keepdims=True)
    if before is not None:
        top = jnp.maximum(before[0], top)
    probs = jnp.exp2((scores - top) * (SCALE * LOG2E))
    total = jnp.sum(probs, axis=0, keepdims=True)
    out = lax.dot_general(val, probs.astype(BF16), (((0,), (0,)), ((), ())), preferred_element_type=F32)
    if before is not None:
        factor = jnp.exp2((before[0] - top) * (SCALE * LOG2E))
        total = total + before[1] * factor
        out = out + before[2] * factor
    return top, total, out


def attend_own_kernel(place, ids_ref, qkv_ref, acc_ref, stat_ref, start_s):
    start_s[...] = document_starts(ids_ref[...]) - place[1] * HALF
    key_iota = lax.broadcasted_iota(jnp.int32, (BK, ROWS), 0)
    diff_iota = key_iota - lax.broadcasted_iota(jnp.int32, (BK, ROWS), 1)
    for at in range(4):
        query = qkv_ref[at, :, 0:128]
        bound = start_s[pl.ds(place[1] * 4 + at, 1), :]

        def put(result, at=at):
            stat_ref[at, 0:1, :], stat_ref[at, 8:9, :], acc_ref[at] = result

        allowed = (key_iota >= bound - at * BK) & (diff_iota <= 0)
        put(softmax_step(query, qkv_ref[at, :, 128:256], qkv_ref[at, :, 256:384], allowed, None))

        def body(i, carry, at=at, query=query, bound=bound, put=put):
            block = at - 1 - i
            before = (stat_ref[at, 0:1, :], stat_ref[at, 8:9, :], acc_ref[at])
            key, val = qkv_ref[block, :, 128:256], qkv_ref[block, :, 256:384]
            put(softmax_step(query, key, val, key_iota >= bound - block * BK, before))
            return carry

        lax.fori_loop(0, at - jnp.maximum(jnp.min(bound), 0) // BK, body, 0)


def attend_own(place, ids, qkv):
    return pl.pallas_call(
        attend_own_kernel,
        grid_spec=pltpu.PrefetchScalarGridSpec(
            num_scalar_prefetch=1,
            grid=(),
            in_specs=vmem_specs(2),
            out_specs=vmem_specs(2),
            scratch_shapes=[pltpu.VMEM((8, ROWS), jnp.int32)],
        ),
        out_shape=[jax.ShapeDtypeStruct((4, 128, ROWS), F32), jax.ShapeDtypeStruct((4, 16, ROWS), F32)],
        name="attend_own",
        compiler_params=pltpu.CompilerParams(vmem_limit_bytes=16 * MIB),
        cost_estimate=pl.CostEstimate(flops=4 * 10**9, bytes_accessed=4 * MIB, transcendentals=4 * 10**6),
    )(place, ids, qkv)


def attend_earlier_kernel(order, place, ids_ref, qkv_ref, *rest):
    cross, (acc_ref, stat_ref) = rest[:4], rest[4:6]
    outs = rest[6 : 6 + len(order)]
    kv_s, start_s, stat_s, acc_s = rest[6 + len(order) :]
    for by in range(4):
        kv_s[lax.rem(place[0] + 4 - by, 4)] = cross[by][...]
    start_s[...] = document_starts(ids_ref[...])
    key_iota = lax.broadcasted_iota(jnp.int32, (BK, ROWS), 0)
    for out, by in zip(outs, order):
        at = lax.rem(place[0] + by, 4)
        query = qkv_ref[at, :, 0:128]
        bound = start_s[pl.ds(place[1] * 4 + at, 1), :]
        stat_s[...] = stat_ref[at]
        acc_s[...] = acc_ref[at]

        def body(i, carry, query=query, bound=bound):
            block = 3 - i
            before = (stat_s[0:1, :], stat_s[8:9, :], acc_s[...])
            result = softmax_step(query, kv_s[block, :, 0:128], kv_s[block, :, 128:256], key_iota >= bound - block * BK, before)
            stat_s[0:1, :], stat_s[8:9, :], acc_s[...] = result
            return carry

        lax.fori_loop(0, place[1] * jnp.maximum(4 - jnp.min(bound) // BK, 0), body, 0)
        out[...] = jnp.transpose(acc_s[...] / stat_s[8:9, :]).astype(BF16)


def attend_earlier(order, place, ids, qkv, cross, acc, stat):
    return pl.pallas_call(
        functools.partial(attend_earlier_kernel, order),
        grid_spec=pltpu.PrefetchScalarGridSpec(
            num_scalar_prefetch=1,
            grid=(),
            in_specs=vmem_specs(8),
            out_specs=vmem_specs(len(order)),
            scratch_shapes=[
                pltpu.VMEM((4, ROWS, 256), BF16),
                pltpu.VMEM((8, ROWS), jnp.int32),
                pltpu.VMEM((16, ROWS), F32),
                pltpu.VMEM((128, ROWS), F32),
            ],
        ),
        out_shape=[jax.ShapeDtypeStruct((ROWS, 128), BF16)] * len(order),
        name="attend_earlier",
        compiler_params=pltpu.CompilerParams(vmem_limit_bytes=16 * MIB),
        cost_estimate=pl.CostEstimate(
            flops=len(order) * 10**9, bytes_accessed=4 * MIB, transcendentals=len(order) * 10**6
        ),
    )(place, ids, qkv, *cross, acc, stat)


BLOCKS = [(0, 1), (1, 1), (2, 1), (3, 1), (2, 0), (1, 0), (3, 0), (0, 0)]


def project_kernel(place, own_ref, sib_ref, w_own, w_sib, *rest):
    a_refs, b_refs = rest[:4], rest[4:6]
    att, weights, staged, in_sem, out_sem, att_sem = rest[6:]
    z = place[0]
    copies = []
    for j, (d, e) in enumerate(BLOCKS):
        block = (lax.rem(place[2] + d, 4) * 2 + lax.rem(place[3] + e, 2)) * 2 + place[4]
        cols = pl.ds(pl.multiple_of(block * 512, 512), 512)
        pair = []
        for i, ref in enumerate((w_own, w_sib)):
            pair.append(pltpu.make_async_copy(ref.at[:, cols], weights.at[j, pl.ds(i * 512, 512), :], in_sem.at[j, i]))
        copies.append(pair)
    loads = []
    for by in range(4):
        col = pl.multiple_of(lax.rem(z + 4 - by, 4) * 128, 128)
        rows = pl.ds(by * ROWS, ROWS)
        for i, ref in enumerate((own_ref, sib_ref)):
            loads.append(pltpu.make_async_copy(ref.at[rows, :], att.at[:, pl.ds(i * 512 + col, 128)], att_sem.at[by, i]))
    for copy in copies[0] + loads + copies[1]:
        copy.start()
    for copy in loads:
        copy.wait()
    stores = []
    for j, (d, e) in enumerate(BLOCKS):
        for copy in copies[j]:
            copy.wait()
        if j + 2 < len(BLOCKS):
            for copy in copies[j + 2]:
                copy.start()
        staged[j] = jnp.dot(att[...], weights[j], preferred_element_type=F32).astype(BF16)
        stores.append(pltpu.make_async_copy(staged.at[j, pl.ds(0, A_ROWS), :], a_refs[d].at[e], out_sem.at[j, 0]))
        stores.append(pltpu.make_async_copy(staged.at[j, pl.ds(A_ROWS, B_ROWS), :], b_refs[e].at[d], out_sem.at[j, 1]))
        stores[-2].start()
        stores[-1].start()
    for copy in stores:
        copy.wait()


def project(place, own, sib, w_own, w_sib):
    anywhere = pl.BlockSpec(memory_space=pl.ANY)
    return pl.pallas_call(
        project_kernel,
        grid_spec=pltpu.PrefetchScalarGridSpec(
            num_scalar_prefetch=1,
            grid=(),
            in_specs=[anywhere] * 4,
            out_specs=[anywhere] * 6,
            scratch_shapes=[
                pltpu.VMEM((ROWS, 1024), BF16),
                pltpu.VMEM((8, 1024, 512), BF16),
                pltpu.VMEM((8, ROWS, 512), BF16),
                pltpu.SemaphoreType.DMA((8, 2)),
                pltpu.SemaphoreType.DMA((8, 2)),
                pltpu.SemaphoreType.DMA((4, 2)),
            ],
        ),
        out_shape=[jax.ShapeDtypeStruct((2, A_ROWS, 512), BF16)] * 4 + [jax.ShapeDtypeStruct((4, B_ROWS, 512), BF16)] * 2,
        name="project",
        compiler_params=pltpu.CompilerParams(vmem_limit_bytes=56 * MIB),
        cost_estimate=pl.CostEstimate(flops=8 * 2 * ROWS * 1024 * 512, bytes_accessed=14 * MIB, transcendentals=0),
    )(place, own, sib, w_own, w_sib)


def hyena_kernel(q_ref, k_ref, v_ref, rim_ref, f_ref, out_ref, sig, shifted, taps):
    for lane in range(4):
        cols = slice(lane * 128, lane * 128 + 128)
        sig[0:128, :] = rim_ref[:, cols].astype(F32)
        product = k_ref[:, cols].astype(F32) * v_ref[:, cols].astype(F32)
        sig[128:640, :] = product.astype(BF16).astype(F32)
        taps[...] = f_ref[:, cols].astype(F32)
        for by in range(8):
            shifted[by, 8:640, :] = sig[8 - by : 640 - by, :]

        def block(b, carry):
            base = 128 + b * 128

            def one_shift(by, acc):
                for high in range(16):
                    tap = taps[pl.ds(high * 8 + by, 1), :]
                    acc = acc + tap * shifted[by, pl.ds(pl.multiple_of(base - high * 8, 8), 128), :]
                return acc

            acc = lax.fori_loop(0, 8, one_shift, jnp.zeros((128, 128), F32))
            rows = pl.ds(pl.multiple_of(b * 128, 128), 128)
            out_ref[rows, cols] = (q_ref[rows, cols].astype(F32) * acc).astype(BF16)
            return carry

        lax.fori_loop(0, 4, block, 0)


def hyena(q, k, v, rim, taps):
    return pl.pallas_call(
        hyena_kernel,
        in_specs=vmem_specs(5),
        out_specs=pl.BlockSpec(memory_space=pltpu.VMEM),
        scratch_shapes=[
            pltpu.VMEM((640, 128), F32),
            pltpu.VMEM((8, 640, 128), F32),
            pltpu.VMEM((128, 128), F32),
        ],
        out_shape=jax.ShapeDtypeStruct((ROWS, 512), BF16),
        name="hyena",
        compiler_params=pltpu.CompilerParams(vmem_limit_bytes=12 * MIB),
        cost_estimate=pl.CostEstimate(flops=10**7, bytes_accessed=3 * 1024, transcendentals=0),
    )(q, k, v, rim, taps)


def add_kernel(keep_ref, one_ref, two_ref, three_ref, send_ref, mine_ref):
    for e, out in ((1, send_ref), (0, mine_ref)):
        total = keep_ref[e].astype(F32) + one_ref[e].astype(F32)
        total = total + two_ref[e].astype(F32) + three_ref[e].astype(F32)
        out[...] = total.astype(out.dtype)


def add_terms(keep, got):
    return pl.pallas_call(
        add_kernel,
        in_specs=vmem_specs(4),
        out_specs=vmem_specs(2),
        out_shape=[jax.ShapeDtypeStruct((A_ROWS, 512), BF16), jax.ShapeDtypeStruct((A_ROWS, 512), F32)],
        name="add_terms",
        compiler_params=pltpu.CompilerParams(vmem_limit_bytes=12 * MIB),
        cost_estimate=pl.CostEstimate(flops=10**10, bytes_accessed=3 * MIB, transcendentals=0),
    )(keep, *got)


def on_device(
    hyena_query,
    hyena_key,
    hyena_value,
    hyena_filter,
    attn_query,
    attn_key,
    attn_value,
    segment_ids,
    out_weight,
):
    ctx = lax.axis_index("ctx")
    head = lax.axis_index("head")
    z = ctx % 4
    x_hi = ctx // 4
    core = head % 2
    place = jnp.stack([z, x_hi, head // 4, (head // 2) % 2, core]).astype(jnp.int32)

    w_sib = lax.ppermute(out_weight, "head", flip_pairs(1))
    packed, *to_cross = pack(attn_query, attn_key, attn_value)
    cross = [lax.ppermute(part, "ctx", cross_pairs(by)) for part, by in zip(to_cross, DIRECT)]
    own = lax.all_to_all(packed, "ctx", 0, 0, axis_index_groups=[[0, 1, 2, 3], [4, 5, 6, 7]])
    forwarded = lax.dynamic_index_in_dim(own, (z + 2) % 4, 0, keepdims=False)[:, 128:]
    cross.insert(2, lax.ppermute(forwarded, "ctx", cross_pairs(0)))

    ids = segment_ids.reshape(8, ROWS)
    late_key, late_value, _ = lax.optimization_barrier((hyena_key[384:], hyena_value[384:], w_sib))
    edge = (late_key.astype(F32) * late_value.astype(F32)).astype(BF16)
    rim = lax.ppermute(edge, "ctx", [(i, i + 1) for i in range(7)])
    acc, stat = attend_own(place, ids, own)
    acc, rim = lax.optimization_barrier((acc, rim))
    attended = attend_earlier((2, 1, 3), place, ids, own, cross, acc, stat)
    back = [lax.ppermute(part, "ctx", z_pairs(by)) for part, by in zip(attended, (2, 1, 3))]
    (kept,) = attend_earlier((0,), place, ids, own, cross, acc, stat)
    mine = jnp.concatenate([kept, back[1], back[0], back[2]], axis=0)
    sib = lax.ppermute(mine, "head", flip_pairs(1))

    *a_terms, b_keep, b_send = project(place, mine, sib, out_weight, w_sib)
    a_keep = a_terms[0]
    b_got = lax.ppermute(b_send, "head", flip_pairs(2))
    a_got = [lax.ppermute(a_terms[d], "head", y_pairs(d)) for d in (2, 1, 3)]
    late_query, _ = lax.optimization_barrier((hyena_query, b_keep))
    hyena_out = hyena(late_query, hyena_key, hyena_value, rim, hyena_filter)
    hyena_out, b_got = lax.optimization_barrier((hyena_out, b_got))

    b_sum = b_keep.astype(F32) + b_got.astype(F32)
    b_parts = [b_sum[d].astype(BF16) for d in range(4)]
    a_got, _ = lax.optimization_barrier((a_got, b_parts))
    b_terms = [lax.ppermute(b_parts[d], "head", y_pairs(d)) for d in (1, 2, 3)]

    a_part, a_mine = add_terms(a_keep, a_got)
    a_term = lax.ppermute(a_part, "head", flip_pairs(2))
    a_final = a_mine + a_term.astype(F32)
    b_final = b_sum[0]
    for term in b_terms:
        b_final = b_final + term.astype(F32)
    stream_a = (hyena_out[:A_ROWS].astype(F32) + a_final).astype(BF16)
    stream_b = (hyena_out[A_ROWS:].astype(F32) + b_final).astype(BF16)
    stream = jnp.concatenate([stream_a, stream_b], axis=0)
    return (hyena_out, stream)


def solution(mesh):
    return jax.shard_map(
        on_device,
        mesh=mesh,
        in_specs=(
            P("ctx", "head"),
            P("ctx", "head"),
            P("ctx", "head"),
            P(None, "head"),
            P("ctx", "head"),
            P("ctx", "head"),
            P("ctx", "head"),
            P(),
            P("head", None),
        ),
        out_specs=(P("ctx", "head"), P("ctx", "head")),
        check_vma=False,
    )
```

```python
import functools
import math

import jax
import jax.numpy as jnp
from jax import lax
from jax.experimental import pallas as pl
from jax.experimental.pallas import tpu as pltpu
from jax.sharding import PartitionSpec as P

HEAD_DIM = 128
ROWS = 512
A_ROWS = 272
B_ROWS = ROWS - A_ROWS
HALF = 2048
BK = 512
SCALE = HEAD_DIM ** -0.5
LOG2E = math.log2(math.e)
F32 = jnp.float32
BF16 = jnp.bfloat16
MIB = 1024 * 1024


def z_pairs(by):
    return [(i, (i // 4) * 4 + (i % 4 + by) % 4) for i in range(8)]


def cross_pairs(by):
    return [(i, 4 + (i + by) % 4) for i in range(4)]


def y_pairs(by):
    return [(i, ((i // 4 + by) % 4) * 4 + i % 4) for i in range(16)]


def flip_pairs(mask):
    return [(i, i ^ mask) for i in range(16)]


def vmem_specs(count):
    return [pl.BlockSpec(memory_space=pltpu.VMEM)] * count


DIRECT = (0, 1, 3)


def pack_kernel(q_ref, k_ref, v_ref, all_ref, *outs):
    for to in range(4):
        for i, ref in enumerate((q_ref, k_ref, v_ref)):
            all_ref[to, :, i * 128 : i * 128 + 128] = ref[:, to * 128 : to * 128 + 128]
    z = lax.rem(lax.axis_index("ctx"), 4)
    for out, by in zip(outs, DIRECT):
        cols = pl.ds(pl.multiple_of(lax.rem(z + by, 4) * 128, 128), 128)
        out[:, 0:128] = k_ref[:, cols]
        out[:, 128:256] = v_ref[:, cols]


def pack(q, k, v):
    return pl.pallas_call(
        pack_kernel,
        in_specs=vmem_specs(3),
        out_specs=vmem_specs(4),
        out_shape=[jax.ShapeDtypeStruct((4, ROWS, 384), BF16)] + [jax.ShapeDtypeStruct((ROWS, 256), BF16)] * 3,
        name="pack",
        compiler_params=pltpu.CompilerParams(vmem_limit_bytes=60 * MIB),
        cost_estimate=pl.CostEstimate(flops=0, bytes_accessed=4 * MIB, transcendentals=0),
    )(q, k, v)


def document_starts(ids):
    starts = jnp.zeros(ids.shape, jnp.int32)
    for value in range(5):
        count = jnp.sum(jnp.where(ids == value, 1.0, 0.0)).astype(jnp.int32)
        starts = starts + jnp.where(ids > value, count, 0)
    return starts


def softmax_step(query, key, val, allowed, before):
    scores = lax.dot_general(key, query, (((1,), (1,)), ((), ())), preferred_element_type=F32)
    scores = jnp.where(allowed, scores, -1e30)
    top = jnp.max(scores, axis=0, keepdims=True)
    if before is not None:
        top = jnp.maximum(before[0], top)
    probs = jnp.exp2((scores - top) * (SCALE * LOG2E))
    total = jnp.sum(probs, axis=0, keepdims=True)
    out = lax.dot_general(val, probs.astype(BF16), (((0,), (0,)), ((), ())), preferred_element_type=F32)
    if before is not None:
        factor = jnp.exp2((before[0] - top) * (SCALE * LOG2E))
        total = total + before[1] * factor
        out = out + before[2] * factor
    return top, total, out


AWAY, HERE = (2, 1, 3), (0,)


def attend_own_kernel(place, ids_ref, qkv_ref, *rest):
    outs, start_s = (rest[0:3], rest[3:6]), rest[6]
    start_s[...] = document_starts(ids_ref[...]) - place[1] * HALF
    key_iota = lax.broadcasted_iota(jnp.int32, (BK, ROWS), 0)
    diff_iota = key_iota - lax.broadcasted_iota(jnp.int32, (BK, ROWS), 1)
    for order, (q_ref, acc_ref, stat_ref) in zip((AWAY, HERE), outs):
        for i, by in enumerate(order):
            at = lax.rem(place[0] + by, 4)
            query = qkv_ref[at, :, 0:128]
            q_ref[i] = query
            bound = start_s[pl.ds(place[1] * 4 + at, 1), :]

            def put(result, i=i, acc_ref=acc_ref, stat_ref=stat_ref):
                stat_ref[i, 0:1, :], stat_ref[i, 8:9, :], acc_ref[i] = result

            allowed = (key_iota >= bound - at * BK) & (diff_iota <= 0)
            put(softmax_step(query, qkv_ref[at, :, 128:256], qkv_ref[at, :, 256:384], allowed, None))

            def body(step, carry, i=i, at=at, query=query, bound=bound, put=put, acc_ref=acc_ref, stat_ref=stat_ref):
                block = at - 1 - step
                before = (stat_ref[i, 0:1, :], stat_ref[i, 8:9, :], acc_ref[i])
                key, val = qkv_ref[block, :, 128:256], qkv_ref[block, :, 256:384]
                put(softmax_step(query, key, val, key_iota >= bound - block * BK, before))
                return carry

            lax.fori_loop(0, at - jnp.maximum(jnp.min(bound), 0) // BK, body, 0)


def attend_own(place, ids, qkv):
    shapes = []
    for order in (AWAY, HERE):
        count = len(order)
        shapes.append(jax.ShapeDtypeStruct((count, ROWS, 128), BF16))
        shapes.append(jax.ShapeDtypeStruct((count, 128, ROWS), F32))
        shapes.append(jax.ShapeDtypeStruct((count, 16, ROWS), F32))
    outs = pl.pallas_call(
        attend_own_kernel,
        grid_spec=pltpu.PrefetchScalarGridSpec(
            num_scalar_prefetch=1,
            grid=(),
            in_specs=vmem_specs(2),
            out_specs=vmem_specs(6),
            scratch_shapes=[pltpu.VMEM((8, ROWS), jnp.int32)],
        ),
        out_shape=shapes,
        name="attend_own",
        compiler_params=pltpu.CompilerParams(vmem_limit_bytes=16 * MIB),
        cost_estimate=pl.CostEstimate(flops=4 * 10**9, bytes_accessed=4 * MIB, transcendentals=4 * 10**6),
    )(place, ids, qkv)
    return outs[0:3], outs[3:6]


def attend_earlier_kernel(order, place, ids_ref, *rest):
    cross, (q_ref, acc_ref, stat_ref) = rest[:4], rest[4:7]
    outs = rest[7 : 7 + len(order)]
    kv_s, start_s, stat_s, acc_s = rest[7 + len(order) :]
    for by in range(4):
        kv_s[lax.rem(place[0] + 4 - by, 4)] = cross[by][...]
    start_s[...] = document_starts(ids_ref[...])
    key_iota = lax.broadcasted_iota(jnp.int32, (BK, ROWS), 0)
    for i, by in enumerate(order):
        at = lax.rem(place[0] + by, 4)
        query = q_ref[i]
        bound = start_s[pl.ds(place[1] * 4 + at, 1), :]
        stat_s[...] = stat_ref[i]
        acc_s[...] = acc_ref[i]

        def body(step, carry, query=query, bound=bound):
            block = 3 - step
            before = (stat_s[0:1, :], stat_s[8:9, :], acc_s[...])
            key, val = kv_s[block, :, 0:128], kv_s[block, :, 128:256]
            result = softmax_step(query, key, val, key_iota >= bound - block * BK, before)
            stat_s[0:1, :], stat_s[8:9, :], acc_s[...] = result
            return carry

        lax.fori_loop(0, place[1] * jnp.maximum(4 - jnp.min(bound) // BK, 0), body, 0)
        outs[i][...] = jnp.transpose(acc_s[...] / stat_s[8:9, :]).astype(BF16)


def attend_earlier(order, place, ids, cross, state):
    return pl.pallas_call(
        functools.partial(attend_earlier_kernel, order),
        grid_spec=pltpu.PrefetchScalarGridSpec(
            num_scalar_prefetch=1,
            grid=(),
            in_specs=vmem_specs(8),
            out_specs=vmem_specs(len(order)),
            scratch_shapes=[
                pltpu.VMEM((4, ROWS, 256), BF16),
                pltpu.VMEM((8, ROWS), jnp.int32),
                pltpu.VMEM((16, ROWS), F32),
                pltpu.VMEM((128, ROWS), F32),
            ],
        ),
        out_shape=[jax.ShapeDtypeStruct((ROWS, 128), BF16)] * len(order),
        name="attend_earlier",
        compiler_params=pltpu.CompilerParams(vmem_limit_bytes=16 * MIB),
        cost_estimate=pl.CostEstimate(flops=len(order) * 10**6, bytes_accessed=4096, transcendentals=0),
    )(place, ids, *cross, *state)


BLOCKS = [(0, 1), (1, 1), (2, 1), (3, 1), (2, 0), (1, 0), (3, 0), (0, 0)]


def project_kernel(place, own_ref, sib_ref, w_own, w_sib, *rest):
    a_refs, b_refs = rest[:4], rest[4:6]
    att, weights, staged, in_sem, out_sem, att_sem = rest[6:]
    z = place[0]
    copies = []
    for j, (d, e) in enumerate(BLOCKS):
        block = (lax.rem(place[2] + d, 4) * 2 + lax.rem(place[3] + e, 2)) * 2 + place[4]
        cols = pl.ds(pl.multiple_of(block * 512, 512), 512)
        pair = []
        for i, ref in enumerate((w_own, w_sib)):
            pair.append(pltpu.make_async_copy(ref.at[:, cols], weights.at[j, pl.ds(i * 512, 512), :], in_sem.at[j, i]))
        copies.append(pair)
    loads = []
    for by in range(4):
        col = pl.multiple_of(lax.rem(z + 4 - by, 4) * 128, 128)
        rows = pl.ds(by * ROWS, ROWS)
        for i, ref in enumerate((own_ref, sib_ref)):
            loads.append(pltpu.make_async_copy(ref.at[rows, :], att.at[:, pl.ds(i * 512 + col, 128)], att_sem.at[by, i]))
    for copy in copies[0] + loads + copies[1]:
        copy.start()
    for copy in loads:
        copy.wait()
    stores = []
    for j, (d, e) in enumerate(BLOCKS):
        for copy in copies[j]:
            copy.wait()
        if j + 2 < len(BLOCKS):
            for copy in copies[j + 2]:
                copy.start()
        staged[j] = jnp.dot(att[...], weights[j], preferred_element_type=F32).astype(BF16)
        stores.append(pltpu.make_async_copy(staged.at[j, pl.ds(0, A_ROWS), :], a_refs[d].at[e], out_sem.at[j, 0]))
        stores.append(pltpu.make_async_copy(staged.at[j, pl.ds(A_ROWS, B_ROWS), :], b_refs[e].at[d], out_sem.at[j, 1]))
        stores[-2].start()
        stores[-1].start()
    for copy in stores:
        copy.wait()


def project(place, own, sib, w_own, w_sib):
    anywhere = pl.BlockSpec(memory_space=pl.ANY)
    return pl.pallas_call(
        project_kernel,
        grid_spec=pltpu.PrefetchScalarGridSpec(
            num_scalar_prefetch=1,
            grid=(),
            in_specs=[anywhere] * 4,
            out_specs=[anywhere] * 6,
            scratch_shapes=[
                pltpu.VMEM((ROWS, 1024), BF16),
                pltpu.VMEM((8, 1024, 512), BF16),
                pltpu.VMEM((8, ROWS, 512), BF16),
                pltpu.SemaphoreType.DMA((8, 2)),
                pltpu.SemaphoreType.DMA((8, 2)),
                pltpu.SemaphoreType.DMA((4, 2)),
            ],
        ),
        out_shape=[jax.ShapeDtypeStruct((2, A_ROWS, 512), BF16)] * 4 + [jax.ShapeDtypeStruct((4, B_ROWS, 512), BF16)] * 2,
        name="project",
        compiler_params=pltpu.CompilerParams(vmem_limit_bytes=52 * MIB),
        cost_estimate=pl.CostEstimate(flops=8 * 2 * ROWS * 1024 * 512, bytes_accessed=14 * MIB, transcendentals=0),
    )(place, own, sib, w_own, w_sib)


def hyena_kernel(q_ref, k_ref, v_ref, rim_ref, f_ref, out_ref, sig, shifted, taps):
    for lane in range(4):
        cols = slice(lane * 128, lane * 128 + 128)
        sig[0:128, :] = rim_ref[:, cols].astype(F32)
        product = k_ref[:, cols].astype(F32) * v_ref[:, cols].astype(F32)
        sig[128:640, :] = product.astype(BF16).astype(F32)
        taps[...] = f_ref[:, cols].astype(F32)
        for by in range(8):
            shifted[by, 8:640, :] = sig[8 - by : 640 - by, :]

        def block(b, carry):
            base = 128 + b * 128

            def one_shift(by, acc):
                for high in range(16):
                    tap = taps[pl.ds(high * 8 + by, 1), :]
                    acc = acc + tap * shifted[by, pl.ds(pl.multiple_of(base - high * 8, 8), 128), :]
                return acc

            acc = lax.fori_loop(0, 8, one_shift, jnp.zeros((128, 128), F32))
            rows = pl.ds(pl.multiple_of(b * 128, 128), 128)
            out_ref[rows, cols] = (q_ref[rows, cols].astype(F32) * acc).astype(BF16)
            return carry

        lax.fori_loop(0, 4, block, 0)


def hyena(q, k, v, rim, taps):
    return pl.pallas_call(
        hyena_kernel,
        in_specs=vmem_specs(5),
        out_specs=pl.BlockSpec(memory_space=pltpu.VMEM),
        scratch_shapes=[
            pltpu.VMEM((640, 128), F32),
            pltpu.VMEM((8, 640, 128), F32),
            pltpu.VMEM((128, 128), F32),
        ],
        out_shape=jax.ShapeDtypeStruct((ROWS, 512), BF16),
        name="hyena",
        compiler_params=pltpu.CompilerParams(vmem_limit_bytes=12 * MIB),
        cost_estimate=pl.CostEstimate(flops=10**7, bytes_accessed=3 * 1024, transcendentals=0),
    )(q, k, v, rim, taps)


def add_kernel(keep_ref, one_ref, two_ref, three_ref, send_ref, mine_ref):
    for e, out in ((1, send_ref), (0, mine_ref)):
        total = keep_ref[e].astype(F32) + one_ref[e].astype(F32)
        total = total + two_ref[e].astype(F32) + three_ref[e].astype(F32)
        out[...] = total.astype(out.dtype)


def add_terms(keep, got):
    return pl.pallas_call(
        add_kernel,
        in_specs=vmem_specs(4),
        out_specs=vmem_specs(2),
        out_shape=[jax.ShapeDtypeStruct((A_ROWS, 512), BF16), jax.ShapeDtypeStruct((A_ROWS, 512), F32)],
        name="add_terms",
        compiler_params=pltpu.CompilerParams(vmem_limit_bytes=12 * MIB),
        cost_estimate=pl.CostEstimate(flops=10**10, bytes_accessed=3 * MIB, transcendentals=0),
    )(keep, *got)


def on_device(
    hyena_query,
    hyena_key,
    hyena_value,
    hyena_filter,
    attn_query,
    attn_key,
    attn_value,
    segment_ids,
    out_weight,
):
    ctx = lax.axis_index("ctx")
    head = lax.axis_index("head")
    z = ctx % 4
    x_hi = ctx // 4
    core = head % 2
    place = jnp.stack([z, x_hi, head // 4, (head // 2) % 2, core]).astype(jnp.int32)

    w_sib = lax.ppermute(out_weight, "head", flip_pairs(1))
    packed, *to_cross = pack(attn_query, attn_key, attn_value)
    cross = [lax.ppermute(part, "ctx", cross_pairs(by)) for part, by in zip(to_cross, DIRECT)]
    own = lax.all_to_all(packed, "ctx", 0, 0, axis_index_groups=[[0, 1, 2, 3], [4, 5, 6, 7]])
    forwarded = lax.dynamic_index_in_dim(own, (z + 2) % 4, 0, keepdims=False)[:, 128:]
    cross.insert(2, lax.ppermute(forwarded, "ctx", cross_pairs(0)))

    ids = segment_ids.reshape(8, ROWS)
    late_key, late_value, _ = lax.optimization_barrier((hyena_key[384:], hyena_value[384:], w_sib))
    edge = (late_key.astype(F32) * late_value.astype(F32)).astype(BF16)
    rim = lax.ppermute(edge, "ctx", [(i, i + 1) for i in range(7)])
    away, here = attend_own(place, ids, own)
    attended = attend_earlier(AWAY, place, ids, cross, away)
    back = [lax.ppermute(part, "ctx", z_pairs(by)) for part, by in zip(attended, AWAY)]
    (kept,) = attend_earlier(HERE, place, ids, cross, here)
    kept, rim = lax.optimization_barrier((kept, rim))
    mine = jnp.concatenate([kept, back[1], back[0], back[2]], axis=0)
    sib = lax.ppermute(mine, "head", flip_pairs(1))

    *a_terms, b_keep, b_send = project(place, mine, sib, out_weight, w_sib)
    a_keep = a_terms[0]
    b_got = lax.ppermute(b_send, "head", flip_pairs(2))
    a_got = [lax.ppermute(a_terms[d], "head", y_pairs(d)) for d in (2, 1, 3)]
    late_query, _ = lax.optimization_barrier((hyena_query, b_keep))
    hyena_out = hyena(late_query, hyena_key, hyena_value, rim, hyena_filter)
    hyena_out, b_got = lax.optimization_barrier((hyena_out, b_got))

    b_sum = b_keep.astype(F32) + b_got.astype(F32)
    b_parts = [b_sum[d].astype(BF16) for d in range(4)]
    a_got, _ = lax.optimization_barrier((a_got, b_parts))
    b_terms = [lax.ppermute(b_parts[d], "head", y_pairs(d)) for d in (1, 2, 3)]

    a_part, a_mine = add_terms(a_keep, a_got)
    a_term = lax.ppermute(a_part, "head", flip_pairs(2))
    a_final = a_mine + a_term.astype(F32)
    b_final = b_sum[0]
    for term in b_terms:
        b_final = b_final + term.astype(F32)
    stream_a = (hyena_out[:A_ROWS].astype(F32) + a_final).astype(BF16)
    stream_b = (hyena_out[A_ROWS:].astype(F32) + b_final).astype(BF16)
    stream = jnp.concatenate([stream_a, stream_b], axis=0)
    return (hyena_out, stream)


def solution(mesh):
    return jax.shard_map(
        on_device,
        mesh=mesh,
        in_specs=(
            P("ctx", "head"),
            P("ctx", "head"),
            P("ctx", "head"),
            P(None, "head"),
            P("ctx", "head"),
            P("ctx", "head"),
            P("ctx", "head"),
            P(),
            P("head", None),
        ),
        out_specs=(P("ctx", "head"), P("ctx", "head")),
        check_vma=False,
    )
```

```python
import functools
import math

import jax
import jax.numpy as jnp
from jax import lax
from jax.experimental import pallas as pl
from jax.experimental.pallas import tpu as pltpu
from jax.sharding import PartitionSpec as P

HEAD_DIM = 128
ROWS = 512
A_ROWS = 272
B_ROWS = ROWS - A_ROWS
HALF = 2048
BK = 512
SCALE = HEAD_DIM ** -0.5
LOG2E = math.log2(math.e)
F32 = jnp.float32
BF16 = jnp.bfloat16
MIB = 1024 * 1024


def z_pairs(by):
    return [(i, (i // 4) * 4 + (i % 4 + by) % 4) for i in range(8)]


def cross_pairs(by):
    return [(i, 4 + (i + by) % 4) for i in range(4)]


def y_pairs(by):
    return [(i, ((i // 4 + by) % 4) * 4 + i % 4) for i in range(16)]


def flip_pairs(mask):
    return [(i, i ^ mask) for i in range(16)]


def vmem_specs(count):
    return [pl.BlockSpec(memory_space=pltpu.VMEM)] * count


def pack_kernel(q_ref, k_ref, v_ref, all_ref, *outs):
    for to in range(4):
        for i, ref in enumerate((q_ref, k_ref, v_ref)):
            all_ref[to, :, i * 128 : i * 128 + 128] = ref[:, to * 128 : to * 128 + 128]
    z = lax.rem(lax.axis_index("ctx"), 4)
    for out, by in zip(outs, (2, 0, 1, 3)):
        cols = pl.ds(pl.multiple_of(lax.rem(z + by, 4) * 128, 128), 128)
        out[:, 0:128] = k_ref[:, cols]
        out[:, 128:256] = v_ref[:, cols]


def pack(q, k, v):
    return pl.pallas_call(
        pack_kernel,
        in_specs=vmem_specs(3),
        out_specs=vmem_specs(5),
        out_shape=[jax.ShapeDtypeStruct((4, ROWS, 384), BF16)] + [jax.ShapeDtypeStruct((ROWS, 256), BF16)] * 4,
        name="pack",
        compiler_params=pltpu.CompilerParams(vmem_limit_bytes=60 * MIB),
        cost_estimate=pl.CostEstimate(flops=0, bytes_accessed=4 * MIB, transcendentals=0),
    )(q, k, v)


def document_starts(ids):
    starts = jnp.zeros(ids.shape, jnp.int32)
    for value in range(5):
        count = jnp.sum(jnp.where(ids == value, 1.0, 0.0)).astype(jnp.int32)
        starts = starts + jnp.where(ids > value, count, 0)
    return starts


def softmax_step(query, key, val, allowed, before):
    scores = lax.dot_general(key, query, (((1,), (1,)), ((), ())), preferred_element_type=F32)
    scores = jnp.where(allowed, scores, -1e30)
    top = jnp.max(scores, axis=0, keepdims=True)
    if before is not None:
        top = jnp.maximum(before[0], top)
    probs = jnp.exp2((scores - top) * (SCALE * LOG2E))
    total = jnp.sum(probs, axis=0, keepdims=True)
    out = lax.dot_general(val, probs.astype(BF16), (((0,), (0,)), ((), ())), preferred_element_type=F32)
    if before is not None:
        factor = jnp.exp2((before[0] - top) * (SCALE * LOG2E))
        total = total + before[1] * factor
        out = out + before[2] * factor
    return top, total, out


AWAY, HERE = (2, 1, 3), (0,)


def attend_own_kernel(place, ids_ref, qkv_ref, *rest):
    outs, start_s = (rest[0:3], rest[3:6]), rest[6]
    start_s[...] = document_starts(ids_ref[...]) - place[1] * HALF
    key_iota = lax.broadcasted_iota(jnp.int32, (BK, ROWS), 0)
    diff_iota = key_iota - lax.broadcasted_iota(jnp.int32, (BK, ROWS), 1)
    for order, (q_ref, acc_ref, stat_ref) in zip((AWAY, HERE), outs):
        for i, by in enumerate(order):
            at = lax.rem(place[0] + by, 4)
            query = qkv_ref[at, :, 0:128]
            q_ref[i] = query
            bound = start_s[pl.ds(place[1] * 4 + at, 1), :]

            def put(result, i=i, acc_ref=acc_ref, stat_ref=stat_ref):
                stat_ref[i, 0:1, :], stat_ref[i, 8:9, :], acc_ref[i] = result

            allowed = (key_iota >= bound - at * BK) & (diff_iota <= 0)
            put(softmax_step(query, qkv_ref[at, :, 128:256], qkv_ref[at, :, 256:384], allowed, None))

            def body(step, carry, i=i, at=at, query=query, bound=bound, put=put, acc_ref=acc_ref, stat_ref=stat_ref):
                block = at - 1 - step
                before = (stat_ref[i, 0:1, :], stat_ref[i, 8:9, :], acc_ref[i])
                key, val = qkv_ref[block, :, 128:256], qkv_ref[block, :, 256:384]
                put(softmax_step(query, key, val, key_iota >= bound - block * BK, before))
                return carry

            lax.fori_loop(0, at - jnp.maximum(jnp.min(bound), 0) // BK, body, 0)


def attend_own(place, ids, qkv):
    shapes = []
    for order in (AWAY, HERE):
        count = len(order)
        shapes.append(jax.ShapeDtypeStruct((count, ROWS, 128), BF16))
        shapes.append(jax.ShapeDtypeStruct((count, 128, ROWS), F32))
        shapes.append(jax.ShapeDtypeStruct((count, 16, ROWS), F32))
    outs = pl.pallas_call(
        attend_own_kernel,
        grid_spec=pltpu.PrefetchScalarGridSpec(
            num_scalar_prefetch=1,
            grid=(),
            in_specs=vmem_specs(2),
            out_specs=vmem_specs(6),
            scratch_shapes=[pltpu.VMEM((8, ROWS), jnp.int32)],
        ),
        out_shape=shapes,
        name="attend_own",
        compiler_params=pltpu.CompilerParams(vmem_limit_bytes=16 * MIB),
        cost_estimate=pl.CostEstimate(flops=4 * 10**9, bytes_accessed=4 * MIB, transcendentals=4 * 10**6),
    )(place, ids, qkv)
    return outs[0:3], outs[3:6]


def attend_earlier_kernel(order, place, ids_ref, *rest):
    cross, (q_ref, acc_ref, stat_ref) = rest[:4], rest[4:7]
    outs = rest[7 : 7 + len(order)]
    kv_s, start_s, stat_s, acc_s = rest[7 + len(order) :]
    for by in range(4):
        kv_s[lax.rem(place[0] + 4 - by, 4)] = cross[by][...]
    start_s[...] = document_starts(ids_ref[...])
    key_iota = lax.broadcasted_iota(jnp.int32, (BK, ROWS), 0)
    for i, by in enumerate(order):
        at = lax.rem(place[0] + by, 4)
        query = q_ref[i]
        bound = start_s[pl.ds(place[1] * 4 + at, 1), :]
        stat_s[...] = stat_ref[i]
        acc_s[...] = acc_ref[i]

        def body(step, carry, query=query, bound=bound):
            block = 3 - step
            before = (stat_s[0:1, :], stat_s[8:9, :], acc_s[...])
            key, val = kv_s[block, :, 0:128], kv_s[block, :, 128:256]
            result = softmax_step(query, key, val, key_iota >= bound - block * BK, before)
            stat_s[0:1, :], stat_s[8:9, :], acc_s[...] = result
            return carry

        lax.fori_loop(0, place[1] * jnp.maximum(4 - jnp.min(bound) // BK, 0), body, 0)
        outs[i][...] = jnp.transpose(acc_s[...] * (1.0 / stat_s[8:9, :])).astype(BF16)


def attend_earlier(order, place, ids, cross, state):
    return pl.pallas_call(
        functools.partial(attend_earlier_kernel, order),
        grid_spec=pltpu.PrefetchScalarGridSpec(
            num_scalar_prefetch=1,
            grid=(),
            in_specs=vmem_specs(8),
            out_specs=vmem_specs(len(order)),
            scratch_shapes=[
                pltpu.VMEM((4, ROWS, 256), BF16),
                pltpu.VMEM((8, ROWS), jnp.int32),
                pltpu.VMEM((16, ROWS), F32),
                pltpu.VMEM((128, ROWS), F32),
            ],
        ),
        out_shape=[jax.ShapeDtypeStruct((ROWS, 128), BF16)] * len(order),
        name="attend_earlier",
        compiler_params=pltpu.CompilerParams(vmem_limit_bytes=16 * MIB),
        cost_estimate=pl.CostEstimate(flops=len(order) * 10**6, bytes_accessed=4096, transcendentals=0),
    )(place, ids, *cross, *state)


BLOCKS = [(0, 1), (1, 1), (2, 1), (3, 1), (2, 0), (1, 0), (3, 0), (0, 0)]


def project_kernel(place, own_ref, sib_ref, w_own, w_sib, *rest):
    a_refs, b_refs = rest[:4], rest[4:6]
    att, weights, staged, in_sem, out_sem, att_sem = rest[6:]
    z = place[0]
    copies = []
    for j, (d, e) in enumerate(BLOCKS):
        block = (lax.rem(place[2] + d, 4) * 2 + lax.rem(place[3] + e, 2)) * 2 + place[4]
        cols = pl.ds(pl.multiple_of(block * 512, 512), 512)
        pair = []
        for i, ref in enumerate((w_own, w_sib)):
            pair.append(pltpu.make_async_copy(ref.at[:, cols], weights.at[j, pl.ds(i * 512, 512), :], in_sem.at[j, i]))
        copies.append(pair)
    loads = []
    for by in range(4):
        col = pl.multiple_of(lax.rem(z + 4 - by, 4) * 128, 128)
        rows = pl.ds(by * ROWS, ROWS)
        for i, ref in enumerate((own_ref, sib_ref)):
            loads.append(pltpu.make_async_copy(ref.at[rows, :], att.at[:, pl.ds(i * 512 + col, 128)], att_sem.at[by, i]))
    for copy in copies[0] + loads + copies[1]:
        copy.start()
    for copy in loads:
        copy.wait()
    stores = []
    for j, (d, e) in enumerate(BLOCKS):
        for copy in copies[j]:
            copy.wait()
        if j + 2 < len(BLOCKS):
            for copy in copies[j + 2]:
                copy.start()
        staged[j] = jnp.dot(att[...], weights[j], preferred_element_type=F32).astype(BF16)
        stores.append(pltpu.make_async_copy(staged.at[j, pl.ds(0, A_ROWS), :], a_refs[d].at[e], out_sem.at[j, 0]))
        stores.append(pltpu.make_async_copy(staged.at[j, pl.ds(A_ROWS, B_ROWS), :], b_refs[e].at[d], out_sem.at[j, 1]))
        stores[-2].start()
        stores[-1].start()
    for copy in stores:
        copy.wait()


def project(place, own, sib, w_own, w_sib):
    anywhere = pl.BlockSpec(memory_space=pl.ANY)
    return pl.pallas_call(
        project_kernel,
        grid_spec=pltpu.PrefetchScalarGridSpec(
            num_scalar_prefetch=1,
            grid=(),
            in_specs=[anywhere] * 4,
            out_specs=[anywhere] * 6,
            scratch_shapes=[
                pltpu.VMEM((ROWS, 1024), BF16),
                pltpu.VMEM((8, 1024, 512), BF16),
                pltpu.VMEM((8, ROWS, 512), BF16),
                pltpu.SemaphoreType.DMA((8, 2)),
                pltpu.SemaphoreType.DMA((8, 2)),
                pltpu.SemaphoreType.DMA((4, 2)),
            ],
        ),
        out_shape=[jax.ShapeDtypeStruct((2, A_ROWS, 512), BF16)] * 4 + [jax.ShapeDtypeStruct((4, B_ROWS, 512), BF16)] * 2,
        name="project",
        compiler_params=pltpu.CompilerParams(vmem_limit_bytes=52 * MIB),
        cost_estimate=pl.CostEstimate(flops=8 * 2 * ROWS * 1024 * 512, bytes_accessed=14 * MIB, transcendentals=0),
    )(place, own, sib, w_own, w_sib)


def hyena_kernel(q_ref, k_ref, v_ref, rim_ref, f_ref, out_ref, sig, shifted, taps):
    for lane in range(4):
        cols = slice(lane * 128, lane * 128 + 128)
        sig[0:128, :] = rim_ref[:, cols].astype(F32)
        product = k_ref[:, cols].astype(F32) * v_ref[:, cols].astype(F32)
        sig[128:640, :] = product.astype(BF16).astype(F32)
        taps[...] = f_ref[:, cols].astype(F32)
        for by in range(8):
            shifted[by, 8:640, :] = sig[8 - by : 640 - by, :]

        def block(b, carry):
            base = 128 + b * 128

            def one_shift(by, acc):
                for high in range(16):
                    tap = taps[pl.ds(high * 8 + by, 1), :]
                    acc = acc + tap * shifted[by, pl.ds(pl.multiple_of(base - high * 8, 8), 128), :]
                return acc

            acc = lax.fori_loop(0, 8, one_shift, jnp.zeros((128, 128), F32))
            rows = pl.ds(pl.multiple_of(b * 128, 128), 128)
            out_ref[rows, cols] = (q_ref[rows, cols].astype(F32) * acc).astype(BF16)
            return carry

        lax.fori_loop(0, 4, block, 0)


def hyena(q, k, v, rim, taps):
    return pl.pallas_call(
        hyena_kernel,
        in_specs=vmem_specs(5),
        out_specs=pl.BlockSpec(memory_space=pltpu.VMEM),
        scratch_shapes=[
            pltpu.VMEM((640, 128), F32),
            pltpu.VMEM((8, 640, 128), F32),
            pltpu.VMEM((128, 128), F32),
        ],
        out_shape=jax.ShapeDtypeStruct((ROWS, 512), BF16),
        name="hyena",
        compiler_params=pltpu.CompilerParams(vmem_limit_bytes=12 * MIB),
        cost_estimate=pl.CostEstimate(flops=10**7, bytes_accessed=3 * 1024, transcendentals=0),
    )(q, k, v, rim, taps)


def add_kernel(keep_ref, one_ref, two_ref, three_ref, send_ref, mine_ref):
    for e, out in ((1, send_ref), (0, mine_ref)):
        total = keep_ref[e].astype(F32) + one_ref[e].astype(F32)
        total = total + two_ref[e].astype(F32) + three_ref[e].astype(F32)
        out[...] = total.astype(out.dtype)


def add_terms(keep, got):
    return pl.pallas_call(
        add_kernel,
        in_specs=vmem_specs(4),
        out_specs=vmem_specs(2),
        out_shape=[jax.ShapeDtypeStruct((A_ROWS, 512), BF16), jax.ShapeDtypeStruct((A_ROWS, 512), F32)],
        name="add_terms",
        compiler_params=pltpu.CompilerParams(vmem_limit_bytes=12 * MIB),
        cost_estimate=pl.CostEstimate(flops=10**10, bytes_accessed=3 * MIB, transcendentals=0),
    )(keep, *got)


def on_device(
    hyena_query,
    hyena_key,
    hyena_value,
    hyena_filter,
    attn_query,
    attn_key,
    attn_value,
    segment_ids,
    out_weight,
):
    ctx = lax.axis_index("ctx")
    head = lax.axis_index("head")
    z = ctx % 4
    x_hi = ctx // 4
    core = head % 2
    place = jnp.stack([z, x_hi, head // 4, (head // 2) % 2, core]).astype(jnp.int32)

    w_sib = lax.ppermute(out_weight, "head", flip_pairs(1))
    packed, far, *near = pack(attn_query, attn_key, attn_value)
    far = lax.ppermute(far, "ctx", [(i, (i + 2) % 4) for i in range(4)])
    cross = [lax.ppermute(part, "ctx", cross_pairs(by)) for part, by in zip(near, (0, 1, 3))]
    own = lax.all_to_all(packed, "ctx", 0, 0, axis_index_groups=[[0, 1, 2, 3], [4, 5, 6, 7]])
    cross.insert(2, lax.ppermute(far, "ctx", cross_pairs(0)))

    ids = segment_ids.reshape(8, ROWS)
    late_key, late_value, _ = lax.optimization_barrier((hyena_key[384:], hyena_value[384:], w_sib))
    edge = (late_key.astype(F32) * late_value.astype(F32)).astype(BF16)
    rim = lax.ppermute(edge, "ctx", [(i, i + 1) for i in range(7)])
    away, here = attend_own(place, ids, own)
    attended = attend_earlier(AWAY, place, ids, cross, away)
    back = [lax.ppermute(part, "ctx", z_pairs(by)) for part, by in zip(attended, AWAY)]
    (kept,) = attend_earlier(HERE, place, ids, cross, here)
    kept, rim = lax.optimization_barrier((kept, rim))
    mine = jnp.concatenate([kept, back[1], back[0], back[2]], axis=0)
    sib = lax.ppermute(mine, "head", flip_pairs(1))

    *a_terms, b_keep, b_send = project(place, mine, sib, out_weight, w_sib)
    a_keep = a_terms[0]
    b_got = lax.ppermute(b_send, "head", flip_pairs(2))
    a_got = [lax.ppermute(a_terms[d], "head", y_pairs(d)) for d in (2, 1, 3)]
    late_query, _ = lax.optimization_barrier((hyena_query, b_keep))
    hyena_out = hyena(late_query, hyena_key, hyena_value, rim, hyena_filter)
    hyena_out, b_got = lax.optimization_barrier((hyena_out, b_got))

    b_sum = b_keep.astype(F32) + b_got.astype(F32)
    b_parts = [b_sum[d].astype(BF16) for d in range(4)]
    a_got, _ = lax.optimization_barrier((a_got, b_parts))
    b_terms = [lax.ppermute(b_parts[d], "head", y_pairs(d)) for d in (1, 2, 3)]

    a_part, a_mine = add_terms(a_keep, a_got)
    a_term = lax.ppermute(a_part, "head", flip_pairs(2))
    a_final = a_mine + a_term.astype(F32)
    b_final = b_sum[0]
    for term in b_terms:
        b_final = b_final + term.astype(F32)
    stream_a = (hyena_out[:A_ROWS].astype(F32) + a_final).astype(BF16)
    stream_b = (hyena_out[A_ROWS:].astype(F32) + b_final).astype(BF16)
    stream = jnp.concatenate([stream_a, stream_b], axis=0)
    return (hyena_out, stream)


def solution(mesh):
    return jax.shard_map(
        on_device,
        mesh=mesh,
        in_specs=(
            P("ctx", "head"),
            P("ctx", "head"),
            P("ctx", "head"),
            P(None, "head"),
            P("ctx", "head"),
            P("ctx", "head"),
            P("ctx", "head"),
            P(),
            P("head", None),
        ),
        out_specs=(P("ctx", "head"), P("ctx", "head")),
        check_vma=False,
    )
```

```python
import functools
import math

import jax
import jax.numpy as jnp
from jax import lax
from jax.experimental import pallas as pl
from jax.experimental.pallas import tpu as pltpu
from jax.sharding import PartitionSpec as P

HEAD_DIM = 128
ROWS = 512
A_ROWS = 272
B_ROWS = ROWS - A_ROWS
HALF = 2048
BK = 512
SCALE = HEAD_DIM ** -0.5
LOG2E = math.log2(math.e)
F32 = jnp.float32
BF16 = jnp.bfloat16
MIB = 1024 * 1024


def z_pairs(by):
    return [(i, (i // 4) * 4 + (i % 4 + by) % 4) for i in range(8)]


def cross_pairs(by):
    return [(i, 4 + (i + by) % 4) for i in range(4)]


def y_pairs(by):
    return [(i, ((i // 4 + by) % 4) * 4 + i % 4) for i in range(16)]


def flip_pairs(mask):
    return [(i, i ^ mask) for i in range(16)]


def vmem_specs(count):
    return [pl.BlockSpec(memory_space=pltpu.VMEM)] * count


def pack_kernel(q_ref, k_ref, v_ref, all_ref, *outs):
    for to in range(4):
        for i, ref in enumerate((q_ref, k_ref, v_ref)):
            all_ref[to, :, i * 128 : i * 128 + 128] = ref[:, to * 128 : to * 128 + 128]
    z = lax.rem(lax.axis_index("ctx"), 4)
    for out, by in zip(outs, (2, 0, 1, 3)):
        cols = pl.ds(pl.multiple_of(lax.rem(z + by, 4) * 128, 128), 128)
        out[:, 0:128] = k_ref[:, cols]
        out[:, 128:256] = v_ref[:, cols]


def pack(q, k, v):
    return pl.pallas_call(
        pack_kernel,
        in_specs=vmem_specs(3),
        out_specs=vmem_specs(5),
        out_shape=[jax.ShapeDtypeStruct((4, ROWS, 384), BF16)] + [jax.ShapeDtypeStruct((ROWS, 256), BF16)] * 4,
        name="pack",
        compiler_params=pltpu.CompilerParams(vmem_limit_bytes=60 * MIB),
        cost_estimate=pl.CostEstimate(flops=0, bytes_accessed=4 * MIB, transcendentals=0),
    )(q, k, v)


def document_starts(ids):
    starts = jnp.zeros(ids.shape, jnp.int32)
    for value in range(5):
        count = jnp.sum(jnp.where(ids == value, 1.0, 0.0)).astype(jnp.int32)
        starts = starts + jnp.where(ids > value, count, 0)
    return starts


def softmax_step(query, key, val, allowed, before):
    scores = lax.dot_general(key, query, (((1,), (1,)), ((), ())), preferred_element_type=F32)
    scores = jnp.where(allowed, scores, -1e30)
    top = jnp.max(scores, axis=0, keepdims=True)
    if before is not None:
        top = jnp.maximum(before[0], top)
    probs = jnp.exp2((scores - top) * (SCALE * LOG2E))
    total = jnp.sum(probs, axis=0, keepdims=True)
    out = lax.dot_general(val, probs.astype(BF16), (((0,), (0,)), ((), ())), preferred_element_type=F32)
    if before is not None:
        factor = jnp.exp2((before[0] - top) * (SCALE * LOG2E))
        total = total + before[1] * factor
        out = out + before[2] * factor
    return top, total, out


AWAY, HERE = (2, 1, 3), (0,)


def attend_own_kernel(place, ids_ref, qkv_ref, *rest):
    outs, start_s = (rest[0:3], rest[3:6]), rest[6]
    start_s[...] = document_starts(ids_ref[...]) - place[1] * HALF
    key_iota = lax.broadcasted_iota(jnp.int32, (BK, ROWS), 0)
    diff_iota = key_iota - lax.broadcasted_iota(jnp.int32, (BK, ROWS), 1)
    for order, (q_ref, acc_ref, stat_ref) in zip((AWAY, HERE), outs):
        for i, by in enumerate(order):
            at = lax.rem(place[0] + by, 4)
            query = qkv_ref[at, :, 0:128]
            q_ref[i] = query
            bound = start_s[pl.ds(place[1] * 4 + at, 1), :]

            def put(result, i=i, acc_ref=acc_ref, stat_ref=stat_ref):
                stat_ref[i, 0:1, :], stat_ref[i, 8:9, :], acc_ref[i] = result

            allowed = (key_iota >= bound - at * BK) & (diff_iota <= 0)
            put(softmax_step(query, qkv_ref[at, :, 128:256], qkv_ref[at, :, 256:384], allowed, None))

            def body(step, carry, i=i, at=at, query=query, bound=bound, put=put, acc_ref=acc_ref, stat_ref=stat_ref):
                block = at - 1 - step
                before = (stat_ref[i, 0:1, :], stat_ref[i, 8:9, :], acc_ref[i])
                key, val = qkv_ref[block, :, 128:256], qkv_ref[block, :, 256:384]
                put(softmax_step(query, key, val, key_iota >= bound - block * BK, before))
                return carry

            lax.fori_loop(0, at - jnp.maximum(jnp.min(bound), 0) // BK, body, 0)


def attend_own(place, ids, qkv):
    shapes = []
    for order in (AWAY, HERE):
        count = len(order)
        shapes.append(jax.ShapeDtypeStruct((count, ROWS, 128), BF16))
        shapes.append(jax.ShapeDtypeStruct((count, 128, ROWS), F32))
        shapes.append(jax.ShapeDtypeStruct((count, 16, ROWS), F32))
    outs = pl.pallas_call(
        attend_own_kernel,
        grid_spec=pltpu.PrefetchScalarGridSpec(
            num_scalar_prefetch=1,
            grid=(),
            in_specs=vmem_specs(2),
            out_specs=vmem_specs(6),
            scratch_shapes=[pltpu.VMEM((8, ROWS), jnp.int32)],
        ),
        out_shape=shapes,
        name="attend_own",
        compiler_params=pltpu.CompilerParams(vmem_limit_bytes=16 * MIB),
        cost_estimate=pl.CostEstimate(flops=4 * 10**9, bytes_accessed=4 * MIB, transcendentals=4 * 10**6),
    )(place, ids, qkv)
    return outs[0:3], outs[3:6]


def attend_earlier_kernel(order, place, ids_ref, *rest):
    cross, (q_ref, acc_ref, stat_ref) = rest[:4], rest[4:7]
    outs = rest[7 : 7 + len(order)]
    kv_s, start_s, stat_s, acc_s = rest[7 + len(order) :]
    for by in range(4):
        kv_s[lax.rem(place[0] + 4 - by, 4)] = cross[by][...]
    start_s[...] = document_starts(ids_ref[...])
    key_iota = lax.broadcasted_iota(jnp.int32, (BK, ROWS), 0)
    for i, by in enumerate(order):
        at = lax.rem(place[0] + by, 4)
        query = q_ref[i]
        bound = start_s[pl.ds(place[1] * 4 + at, 1), :]
        stat_s[...] = stat_ref[i]
        acc_s[...] = acc_ref[i]

        def body(step, carry, query=query, bound=bound):
            block = 3 - step
            before = (stat_s[0:1, :], stat_s[8:9, :], acc_s[...])
            key, val = kv_s[block, :, 0:128], kv_s[block, :, 128:256]
            result = softmax_step(query, key, val, key_iota >= bound - block * BK, before)
            stat_s[0:1, :], stat_s[8:9, :], acc_s[...] = result
            return carry

        lax.fori_loop(0, place[1] * jnp.maximum(4 - jnp.min(bound) // BK, 0), body, 0)
        outs[i][...] = jnp.transpose(acc_s[...] * (1.0 / stat_s[8:9, :])).astype(BF16)


def attend_earlier(order, place, ids, cross, state):
    return pl.pallas_call(
        functools.partial(attend_earlier_kernel, order),
        grid_spec=pltpu.PrefetchScalarGridSpec(
            num_scalar_prefetch=1,
            grid=(),
            in_specs=vmem_specs(8),
            out_specs=vmem_specs(len(order)),
            scratch_shapes=[
                pltpu.VMEM((4, ROWS, 256), BF16),
                pltpu.VMEM((8, ROWS), jnp.int32),
                pltpu.VMEM((16, ROWS), F32),
                pltpu.VMEM((128, ROWS), F32),
            ],
        ),
        out_shape=[jax.ShapeDtypeStruct((ROWS, 128), BF16)] * len(order),
        name="attend_earlier",
        compiler_params=pltpu.CompilerParams(vmem_limit_bytes=16 * MIB),
        cost_estimate=pl.CostEstimate(flops=len(order) * 10**6, bytes_accessed=4096, transcendentals=0),
    )(place, ids, *cross, *state)


BLOCKS = [(0, 1), (1, 1), (2, 1), (3, 1), (2, 0), (1, 0), (3, 0), (0, 0)]


def project_kernel(place, own_ref, sib_ref, w_own, w_sib, *rest):
    a_refs, b_refs = rest[:4], rest[4:6]
    att, weights, staged, in_sem, out_sem, att_sem = rest[6:]
    z = place[0]
    copies = []
    for j, (d, e) in enumerate(BLOCKS):
        block = (lax.rem(place[2] + d, 4) * 2 + lax.rem(place[3] + e, 2)) * 2 + place[4]
        cols = pl.ds(pl.multiple_of(block * 512, 512), 512)
        pair = []
        for i, ref in enumerate((w_own, w_sib)):
            pair.append(pltpu.make_async_copy(ref.at[:, cols], weights.at[j, pl.ds(i * 512, 512), :], in_sem.at[j, i]))
        copies.append(pair)
    loads = []
    for by in range(4):
        col = pl.multiple_of(lax.rem(z + 4 - by, 4) * 128, 128)
        rows = pl.ds(by * ROWS, ROWS)
        for i, ref in enumerate((own_ref, sib_ref)):
            loads.append(pltpu.make_async_copy(ref.at[rows, :], att.at[:, pl.ds(i * 512 + col, 128)], att_sem.at[by, i]))
    for copy in copies[0] + loads + copies[1]:
        copy.start()
    for copy in loads:
        copy.wait()
    stores = []
    for j, (d, e) in enumerate(BLOCKS):
        for copy in copies[j]:
            copy.wait()
        if j + 2 < len(BLOCKS):
            for copy in copies[j + 2]:
                copy.start()
        staged[j] = jnp.dot(att[...], weights[j], preferred_element_type=F32).astype(BF16)
        stores.append(pltpu.make_async_copy(staged.at[j, pl.ds(0, A_ROWS), :], a_refs[d].at[e], out_sem.at[j, 0]))
        stores.append(pltpu.make_async_copy(staged.at[j, pl.ds(A_ROWS, B_ROWS), :], b_refs[e].at[d], out_sem.at[j, 1]))
        stores[-2].start()
        stores[-1].start()
    for copy in stores:
        copy.wait()


def project(place, own, sib, w_own, w_sib):
    anywhere = pl.BlockSpec(memory_space=pl.ANY)
    return pl.pallas_call(
        project_kernel,
        grid_spec=pltpu.PrefetchScalarGridSpec(
            num_scalar_prefetch=1,
            grid=(),
            in_specs=[anywhere] * 4,
            out_specs=[anywhere] * 6,
            scratch_shapes=[
                pltpu.VMEM((ROWS, 1024), BF16),
                pltpu.VMEM((8, 1024, 512), BF16),
                pltpu.VMEM((8, ROWS, 512), BF16),
                pltpu.SemaphoreType.DMA((8, 2)),
                pltpu.SemaphoreType.DMA((8, 2)),
                pltpu.SemaphoreType.DMA((4, 2)),
            ],
        ),
        out_shape=[jax.ShapeDtypeStruct((2, A_ROWS, 512), BF16)] * 4 + [jax.ShapeDtypeStruct((4, B_ROWS, 512), BF16)] * 2,
        name="project",
        compiler_params=pltpu.CompilerParams(vmem_limit_bytes=52 * MIB),
        cost_estimate=pl.CostEstimate(flops=8 * 2 * ROWS * 1024 * 512, bytes_accessed=14 * MIB, transcendentals=0),
    )(place, own, sib, w_own, w_sib)


def hyena_kernel(q_ref, k_ref, v_ref, rim_ref, f_ref, out_ref, sig, shifted, taps):
    for lane in range(4):
        cols = slice(lane * 128, lane * 128 + 128)
        sig[0:128, :] = rim_ref[:, cols].astype(F32)
        product = k_ref[:, cols].astype(F32) * v_ref[:, cols].astype(F32)
        sig[128:640, :] = product.astype(BF16).astype(F32)
        taps[...] = f_ref[:, cols].astype(F32)
        for by in range(8):
            shifted[by, 8:640, :] = sig[8 - by : 640 - by, :]

        def block(b, carry):
            base = 128 + b * 128

            def one_shift(by, acc):
                for high in range(16):
                    tap = taps[pl.ds(high * 8 + by, 1), :]
                    acc = acc + tap * shifted[by, pl.ds(pl.multiple_of(base - high * 8, 8), 128), :]
                return acc

            acc = lax.fori_loop(0, 8, one_shift, jnp.zeros((128, 128), F32))
            rows = pl.ds(pl.multiple_of(b * 128, 128), 128)
            out_ref[rows, cols] = (q_ref[rows, cols].astype(F32) * acc).astype(BF16)
            return carry

        lax.fori_loop(0, 4, block, 0)


def hyena(q, k, v, rim, taps):
    return pl.pallas_call(
        hyena_kernel,
        in_specs=vmem_specs(5),
        out_specs=pl.BlockSpec(memory_space=pltpu.VMEM),
        scratch_shapes=[
            pltpu.VMEM((640, 128), F32),
            pltpu.VMEM((8, 640, 128), F32),
            pltpu.VMEM((128, 128), F32),
        ],
        out_shape=jax.ShapeDtypeStruct((ROWS, 512), BF16),
        name="hyena",
        compiler_params=pltpu.CompilerParams(vmem_limit_bytes=12 * MIB),
        cost_estimate=pl.CostEstimate(flops=10**7, bytes_accessed=3 * 1024, transcendentals=0),
    )(q, k, v, rim, taps)


def add_kernel(keep_ref, one_ref, two_ref, three_ref, send_ref, mine_ref):
    for e, out in ((1, send_ref), (0, mine_ref)):
        total = keep_ref[e].astype(F32) + one_ref[e].astype(F32)
        total = total + two_ref[e].astype(F32) + three_ref[e].astype(F32)
        out[...] = total.astype(out.dtype)


def add_terms(keep, got):
    return pl.pallas_call(
        add_kernel,
        in_specs=vmem_specs(4),
        out_specs=vmem_specs(2),
        out_shape=[jax.ShapeDtypeStruct((A_ROWS, 512), BF16), jax.ShapeDtypeStruct((A_ROWS, 512), F32)],
        name="add_terms",
        compiler_params=pltpu.CompilerParams(vmem_limit_bytes=12 * MIB),
        cost_estimate=pl.CostEstimate(flops=10**10, bytes_accessed=3 * MIB, transcendentals=0),
    )(keep, *got)


def on_device(
    hyena_query,
    hyena_key,
    hyena_value,
    hyena_filter,
    attn_query,
    attn_key,
    attn_value,
    segment_ids,
    out_weight,
):
    ctx = lax.axis_index("ctx")
    head = lax.axis_index("head")
    z = ctx % 4
    x_hi = ctx // 4
    core = head % 2
    place = jnp.stack([z, x_hi, head // 4, (head // 2) % 2, core]).astype(jnp.int32)

    w_sib = lax.ppermute(out_weight, "head", flip_pairs(1))
    packed, far, *near = pack(attn_query, attn_key, attn_value)
    far = lax.ppermute(far, "ctx", [(i, (i + 2) % 4) for i in range(4)])
    cross = [lax.ppermute(part, "ctx", cross_pairs(by)) for part, by in zip(near, (0, 1, 3))]
    own = lax.all_to_all(packed, "ctx", 0, 0, axis_index_groups=[[0, 1, 2, 3], [4, 5, 6, 7]])
    cross.insert(2, lax.ppermute(far, "ctx", cross_pairs(0)))

    ids = segment_ids.reshape(8, ROWS)
    late_key, late_value, _ = lax.optimization_barrier((hyena_key[384:], hyena_value[384:], w_sib))
    edge = (late_key.astype(F32) * late_value.astype(F32)).astype(BF16)
    rim = lax.ppermute(edge, "ctx", [(i, i + 1) for i in range(7)])
    away, here = attend_own(place, ids, own)
    attended = attend_earlier(AWAY, place, ids, cross, away)
    back = [lax.ppermute(part, "ctx", z_pairs(by)) for part, by in zip(attended, AWAY)]
    (kept,) = attend_earlier(HERE, place, ids, cross, here)
    kept, rim = lax.optimization_barrier((kept, rim))
    mine = jnp.concatenate([kept, back[1], back[0], back[2]], axis=0)
    sib = lax.ppermute(mine, "head", flip_pairs(1))

    *a_terms, b_keep, b_send = project(place, mine, sib, out_weight, w_sib)
    a_keep = a_terms[0]
    b_got = lax.ppermute(b_send, "head", flip_pairs(2))
    a_got = [lax.ppermute(a_terms[d], "head", y_pairs(d)) for d in (2, 1, 3)]
    late_query, _ = lax.optimization_barrier((hyena_query, b_keep))
    hyena_out = hyena(late_query, hyena_key, hyena_value, rim, hyena_filter)
    hyena_out, b_got = lax.optimization_barrier((hyena_out, b_got))

    b_sum = b_keep.astype(F32) + b_got.astype(F32)
    b_parts = [b_sum[d].astype(BF16) for d in range(4)]
    a_got, _ = lax.optimization_barrier((a_got, b_parts))
    b_terms = [lax.ppermute(b_parts[d], "head", y_pairs(d)) for d in (1, 2, 3)]

    a_part, a_mine = add_terms(a_keep, a_got)
    a_term = lax.ppermute(a_part, "head", flip_pairs(2))
    a_final = a_mine + a_term.astype(F32)
    b_final = lax.optimization_barrier(hyena_out[A_ROWS:].astype(F32) + b_sum[0])
    for term in b_terms:
        b_final = b_final + term.astype(F32)
    stream_a = (hyena_out[:A_ROWS].astype(F32) + a_final).astype(BF16)
    stream_b = b_final.astype(BF16)
    stream = jnp.concatenate([stream_a, stream_b], axis=0)
    return (hyena_out, stream)


def solution(mesh):
    return jax.shard_map(
        on_device,
        mesh=mesh,
        in_specs=(
            P("ctx", "head"),
            P("ctx", "head"),
            P("ctx", "head"),
            P(None, "head"),
            P("ctx", "head"),
            P("ctx", "head"),
            P("ctx", "head"),
            P(),
            P("head", None),
        ),
        out_specs=(P("ctx", "head"), P("ctx", "head")),
        check_vma=False,
    )
```
